256 devices in a mesh: rows: 8 (over y, core), labels: 32 (over x, z).
Axes of the slice: x: 4, y: 4, z: 8, core: 2. Of those that a mesh axis runs over, the one named last changes fastest.
Arguments:
- embeddings: bfloat16 [8192, 768], P(('rows', 'labels')), may hold values from -6 to 6
- class_weight: bfloat16 [65536, 768], P('labels'), may hold values from -0.4375 to 0.4375
- class_bias: float32 [65536], P('labels'), may hold values from -10 to -8
- propensity: float32 [65536], P('labels'), may hold values from 0.1 to 0.9
- label_ids: int32 [8192, 32], P('rows'), may hold values from 0 to 65535
- label_count: int32 [8192], P('rows'), may hold values from 1 to 32
- label_bins: int32 [65536], P('labels'), may hold values from 0 to 15
- prior_mean: float32 [16], replicated, may hold values from 0.1 to 0.9
Outputs:
- new_propensity: float32 [65536], P('labels')
- weight_grad: bfloat16 [65536, 768], P('labels', 'rows')
- embed_grad: bfloat16 [8192, 768], P(('rows', 'labels'))
The draws below stay inside these ranges and needn't reach their ends.
Inputs may be any that keep to these rules, and one draw needn't show every extreme that they name: `label_ids`: entries past a row's count are padding and are ignored; ids may repeat.
All inputs are finite; a program needn't handle non-finite values.
Results may differ from the reference program's by a relative error of at most 0.014.
Values may be sent and summed in bfloat16 or wider, within the bound.
No kernel may reach another device: no remote copies, remote signals or barrier semaphores. Data moves between devices by JAX's collectives and lax.ppermute only.
A program may use at most 64 MiB of HBM per device.

```python
import jax
import jax.numpy as jnp
from jax import lax

D = 768
LAB_DEV = 2048
MAXOBS = 32
BINS = 16
ROWS_GRP = 1024
ROWS = 8192
LABELS = 65536
N_ROWS = 8
N_LABELS = 32


def touch_ends(entries, own_key, least, largest):
    dims = entries.shape
    place = [jax.random.randint(jax.random.fold_in(own_key, axis), (), 0, dims[axis]) for axis in range(len(dims))]
    entries = entries.at[tuple(place)].set(least)
    longest = dims.index(max(dims))
    place[longest] = (place[longest] + 1) % dims[longest]
    return entries.at[tuple(place)].set(largest)


def block_scale(own_key, extent, split, low, top_value):
    gain = 1.0
    for position, blocks in split:
        draws = jax.random.uniform(jax.random.fold_in(jax.random.fold_in(own_key, 6), position), (blocks,), jnp.float32, low / len(split), top_value / len(split))
        gain = gain * jnp.repeat(jnp.exp(draws), extent[position] // blocks).reshape((-1,) + (1,) * (len(extent) - 1 - position))
    return gain


def centred(rng, extent, deviation, limit, cuts=(), kind=jnp.bfloat16):
    result = jax.random.normal(rng, extent, jnp.float32) * deviation
    if len(cuts) > 0:
        result = block_scale(rng, extent, cuts, -0.22, 0.18) * result
    return jnp.clip(result, min=-limit, max=limit).astype(kind)


def setup_inputs(seed: int = 0) -> dict:
    streams_of = jax.random.split(jax.random.key(seed), 9)
    embeddings = centred(streams_of[0], (ROWS, D), 1.0, 6.0, ((0, 256),))
    class_weight = centred(streams_of[1], (LABELS, D), (D // 4) ** -0.5, 0.4375, ((0, 32),))
    class_bias = jnp.clip(-10.0 + 2.0 * jax.random.uniform(streams_of[2], (LABELS,), jnp.float32) ** block_scale(streams_of[2], (LABELS,), ((0, 32),), -0.2, 0.2), -10.0, -8.0)
    propensity = jnp.clip(0.1 + 0.79999997 * jax.random.uniform(streams_of[3], (LABELS,), jnp.float32) ** block_scale(streams_of[3], (LABELS,), ((0, 32),), -0.2, 0.2), 0.1, 0.9)
    label_ids = touch_ends(jax.random.randint(streams_of[4], (ROWS, MAXOBS), 0, LABELS), jax.random.fold_in(streams_of[4], 1), 0, LABELS - 1).astype(jnp.int32)
    label_count = touch_ends(jax.random.randint(streams_of[5], (ROWS,), 1, MAXOBS + 1), jax.random.fold_in(streams_of[5], 1), 1, MAXOBS).astype(jnp.int32)
    label_bins = touch_ends(jax.random.randint(streams_of[6], (LABELS,), 0, BINS), jax.random.fold_in(streams_of[6], 1), 0, BINS - 1).astype(jnp.int32)
    prior_mean = jnp.clip(jax.random.uniform(streams_of[7], (BINS,), jnp.float32, 0.1, 0.9), 0.1, 0.9)
    return {"embeddings": embeddings, "class_weight": class_weight, "class_bias": class_bias, "propensity": propensity, "label_ids": label_ids, "label_count": label_count, "label_bins": label_bins, "prior_mean": prior_mean}


def reference(embeddings, class_weight, class_bias, propensity, label_ids, label_count, label_bins, prior_mean):
    slots = jnp.arange(MAXOBS, dtype=jnp.int32)
    live = slots[None, :] < label_count[:, None]
    row_index = jnp.broadcast_to(jnp.arange(ROWS, dtype=jnp.int32)[:, None], (ROWS, MAXOBS))
    grouped = embeddings.reshape(N_ROWS, ROWS_GRP, D).astype(jnp.float32)

    def block(carry, shard):
        start = (shard * LAB_DEV).astype(jnp.int32)
        weight = lax.dynamic_slice_in_dim(class_weight, start, LAB_DEV, 0)
        bias = lax.dynamic_slice_in_dim(class_bias, start, LAB_DEV, 0)
        prop = lax.dynamic_slice_in_dim(propensity, start, LAB_DEV, 0)
        bins = lax.dynamic_slice_in_dim(label_bins, start, LAB_DEV, 0)
        scores = lax.dot_general(embeddings, weight, (((1,), (1,)), ((), ())), preferred_element_type=jnp.float32) + bias[None, :]
        prob = jax.nn.sigmoid(scores)
        local = label_ids - start
        valid = live & (local >= 0) & (local < LAB_DEV)
        column = jnp.where(valid, local, LAB_DEV).astype(jnp.int32)
        observed = jnp.zeros((ROWS, LAB_DEV), jnp.float32).at[row_index, column].set(1.0, mode="drop")
        posterior = observed + (1.0 - observed) * prob * (1.0 - prop[None, :]) / (1.0 - prob * prop[None, :])
        post_sum = jnp.sum(posterior, axis=0)
        obs_sum = jnp.sum(observed, axis=0)
        updated = (obs_sum + 8.0 * prior_mean[bins]) / (post_sum + 8.0)
        residual_grad = (prob - posterior).astype(jnp.bfloat16)
        parts = jnp.einsum("grl,grd->gld", residual_grad.reshape(N_ROWS, ROWS_GRP, LAB_DEV).astype(jnp.float32), grouped)
        parts = lax.optimization_barrier(parts.astype(jnp.bfloat16)).astype(jnp.float32)
        summed = jnp.sum(parts, axis=0)
        wgrad = (summed / updated[:, None]).astype(jnp.bfloat16)
        scaled = (weight.astype(jnp.float32) / updated[:, None]).astype(jnp.bfloat16)
        term = jnp.dot(residual_grad, scaled, preferred_element_type=jnp.float32)
        term = lax.optimization_barrier(term.astype(jnp.bfloat16)).astype(jnp.float32)
        carry = carry + term
        return carry, (updated, wgrad)

    total, outs = lax.scan(block, jnp.zeros((ROWS, D), jnp.float32), jnp.arange(N_LABELS, dtype=jnp.int32))
    updated, wgrad = outs
    return updated.reshape(LABELS), wgrad.reshape(LABELS, D), total.astype(jnp.bfloat16)
```

```python
import functools

import jax
import jax.numpy as jnp
from jax import lax
from jax.experimental import pallas as pl
from jax.experimental.pallas import tpu as pltpu
from jax.sharding import Mesh, PartitionSpec as P

BF = jnp.bfloat16
F32 = jnp.float32
LANES = 128


def ring(n, d):
    return [(i, (i + d) % n) for i in range(n)]


def observed_words(label_ids, label_count, offset, width):
    slots = jnp.arange(label_ids.shape[1], dtype=jnp.int32)
    local = label_ids - offset
    valid = (slots[None, :] < label_count[:, None]) & (local >= 0) & (local < width)
    lane = jnp.where(valid, local & (LANES - 1), -1)
    word = jnp.left_shift(jnp.int32(1), jnp.where(valid, local >> 7, 0))
    lanes = jnp.arange(LANES, dtype=jnp.int32)
    hits = jnp.where(lane[:, :, None] == lanes[None, None, :], word[:, :, None], 0)
    return lax.reduce(hits, jnp.int32(0), lax.bitwise_or, (1,))


def score_kernel(x_ref, w_ref, bias_ref, prop_ref, words_ref, res_ref, post_ref, *, chunk):
    tile = w_ref.shape[0]
    step = pl.program_id(0)
    first = step * (tile // LANES)
    bias = bias_ref[...]
    prop = prop_ref[...]
    rest = 1.0 - prop
    total = jnp.zeros((8, tile), F32)
    for start in range(0, x_ref.shape[0], chunk):
        rows = slice(start, start + chunk)
        scores = (
            lax.dot_general(
                x_ref[rows, :], w_ref[...], (((1,), (1,)), ((), ())), preferred_element_type=F32
            )
            + bias
        )
        grown = 1.0 + jnp.exp(jnp.minimum(-scores, 88.0))
        prob = 1.0 / grown
        unseen = rest / (grown - prop)
        words = words_ref[rows, :]
        seen = jnp.concatenate(
            [words & jnp.left_shift(jnp.int32(1), first + b) for b in range(tile // LANES)], axis=1
        )
        posterior = jnp.where(seen != 0, 1.0, unseen)
        res_ref[rows, :] = (prob - posterior).astype(BF)
        total = total + jnp.sum(posterior.reshape(chunk // 8, 8, tile), axis=0)
    post_ref[...] = jnp.sum(total, axis=0, keepdims=True)


def score_call(x, w, bias, prop, words, tile=512, chunk=256):
    rows, depth = x.shape
    width = w.shape[0]
    return pl.pallas_call(
        functools.partial(score_kernel, chunk=chunk),
        grid=(width // tile,),
        in_specs=[
            pl.BlockSpec((rows, depth), lambda i: (0, 0)),
            pl.BlockSpec((tile, depth), lambda i: (i, 0)),
            pl.BlockSpec((1, tile), lambda i: (0, i)),
            pl.BlockSpec((1, tile), lambda i: (0, i)),
            pl.BlockSpec((rows, LANES), lambda i: (0, 0)),
        ],
        out_specs=[
            pl.BlockSpec((rows, tile), lambda i: (0, i)),
            pl.BlockSpec((1, tile), lambda i: (0, i)),
        ],
        out_shape=[
            jax.ShapeDtypeStruct((rows, width), BF),
            jax.ShapeDtypeStruct((1, width), F32),
        ],
        cost_estimate=pl.CostEstimate(
            flops=2 * rows * width * depth,
            bytes_accessed=2 * (rows * depth + width * depth + rows * width),
            transcendentals=3 * rows * width,
        ),
        name="scores",
    )(x, w, bias, prop, words)


def sum_rows(v):
    v = v + lax.ppermute(v, "core", ring(2, 1))
    one, two, three = (lax.ppermute(v, "y", ring(4, d)) for d in (1, 2, 3))
    return (v + two) + (one + three)


def scatter_weights(terms):
    core, y = lax.axis_index("core"), lax.axis_index("y")
    given = lax.dynamic_index_in_dim(terms, 1 - core, 1, keepdims=False)
    kept = lax.dynamic_index_in_dim(terms, core, 1, keepdims=False)
    pair = kept.astype(F32) + lax.ppermute(given, "core", ring(2, 1)).astype(F32)
    pair = pair.astype(BF)
    total = lax.dynamic_index_in_dim(pair, y, 0, keepdims=False).astype(F32)
    for d in (1, 2, 3):
        block = lax.dynamic_index_in_dim(pair, (y + d) % 4, 0, keepdims=False)
        total = total + lax.ppermute(block, "y", ring(4, d)).astype(F32)
    return total


def bin_prior(bins, prior_mean):
    levels = jnp.arange(prior_mean.shape[0], dtype=jnp.int32)
    onehot = (bins[:, None] == levels[None, :]).astype(F32)
    return jnp.sum(onehot * prior_mean[None, :], axis=1)


def body(
    embeddings, class_weight, class_bias, propensity, label_ids, label_count, label_bins, prior_mean
):
    width, depth = class_weight.shape
    part = embeddings.shape[0]
    nx, nz = 4, 8
    offset = (lax.axis_index("x") * nz + lax.axis_index("z")) * width

    along_z = lax.all_to_all(
        jnp.tile(embeddings, (nz, 1)), "z", split_axis=0, concat_axis=0, tiled=True
    )
    x_all = lax.all_to_all(
        jnp.tile(along_z, (nx, 1)), "x", split_axis=0, concat_axis=0, tiled=True
    )

    words = observed_words(label_ids, label_count, offset, width)
    bits = jnp.arange(width // LANES, dtype=jnp.int32)
    seen = (words[:, None, :] >> bits[None, :, None]) & 1
    obs_sum = sum_rows(jnp.sum(seen.astype(F32), axis=0).reshape(1, width))
    prior = bin_prior(label_bins, prior_mean)

    x_all, obs_sum = lax.optimization_barrier((x_all, obs_sum))
    residual, post = score_call(
        x_all, class_weight, class_bias[None, :], propensity[None, :], words
    )
    post_sum = sum_rows(post)
    updated = ((obs_sum + 8.0 * prior[None, :]) / (post_sum + 8.0)).reshape(width)

    weight_terms = lax.dot_general(
        x_all, residual, (((0,), (0,)), ((), ())), preferred_element_type=F32
    ).astype(BF)
    weight_sum = scatter_weights(weight_terms.reshape(4, 2, depth // 8, width))
    weight_grad = (weight_sum / updated[None, :]).astype(BF).T

    scaled_weight = (class_weight.astype(F32) / updated[:, None]).astype(BF)
    embed_terms = jnp.dot(residual, scaled_weight, preferred_element_type=F32).astype(BF)
    embed_parts = lax.all_to_all(
        embed_terms, ("x", "z"), split_axis=0, concat_axis=0, tiled=True
    )
    embed_grad = jnp.sum(embed_parts.reshape(nx * nz, part, depth).astype(F32), axis=0).astype(BF)
    return updated, weight_grad, embed_grad


def solution(mesh):
    fine = Mesh(mesh.devices.reshape(4, 2, 4, 8), ("y", "core", "x", "z"))
    rows, labels = ("y", "core"), ("x", "z")
    both = rows + labels
    return jax.shard_map(
        body,
        mesh=fine,
        in_specs=(
            P(both, None),
            P(labels, None),
            P(labels),
            P(labels),
            P(rows, None),
            P(rows),
            P(labels),
            P(),
        ),
        out_specs=(P(labels), P(labels, rows), P(both, None)),
        check_vma=False,
    )
```

```python
import functools

import jax
import jax.numpy as jnp
from jax import lax
from jax.experimental import pallas as pl
from jax.experimental.pallas import tpu as pltpu
from jax.sharding import Mesh, PartitionSpec as P

BF = jnp.bfloat16
F32 = jnp.float32
LANES = 128
NX, NZ, NY, NC = 4, 8, 4, 2


def ring(n, d):
    return [(i, (i + d) % n) for i in range(n)]


def observed_words(label_ids, label_count, offset, width):
    slots = jnp.arange(label_ids.shape[1], dtype=jnp.int32)
    local = label_ids - offset
    valid = (slots[None, :] < label_count[:, None]) & (local >= 0) & (local < width)
    lane = jnp.where(valid, local & (LANES - 1), -1)
    word = jnp.left_shift(jnp.int32(1), jnp.where(valid, local >> 7, 0))
    lanes = jnp.arange(LANES, dtype=jnp.int32)
    hits = jnp.where(lane[:, :, None] == lanes[None, None, :], word[:, :, None], 0)
    return lax.reduce(hits, jnp.int32(0), lax.bitwise_or, (1,))


def score_kernel(x_ref, w_ref, bias_ref, prop_ref, words_ref, res_ref, post_ref, *, chunk):
    tile = w_ref.shape[0]
    step = pl.program_id(0)
    first = step * (tile // LANES)
    bias = bias_ref[...]
    prop = prop_ref[...]
    rest = 1.0 - prop
    total = jnp.zeros((8, tile), F32)
    for start in range(0, x_ref.shape[0], chunk):
        rows = slice(start, start + chunk)
        scores = (
            lax.dot_general(
                x_ref[rows, :], w_ref[...], (((1,), (1,)), ((), ())), preferred_element_type=F32
            )
            + bias
        )
        grown = 1.0 + jnp.exp(jnp.minimum(-scores, 88.0))
        prob = 1.0 / grown
        unseen = rest / (grown - prop)
        words = words_ref[rows, :]
        seen = jnp.concatenate(
            [words & jnp.left_shift(jnp.int32(1), first + b) for b in range(tile // LANES)], axis=1
        )
        posterior = jnp.where(seen != 0, 1.0, unseen)
        res_ref[rows, :] = (prob - posterior).astype(BF)
        total = total + jnp.sum(posterior.reshape(chunk // 8, 8, tile), axis=0)
    post_ref[...] = jnp.sum(total, axis=0, keepdims=True)


def score_call(x, w, bias, prop, words, tile=512, chunk=256):
    rows, depth = x.shape
    width = w.shape[0]
    return pl.pallas_call(
        functools.partial(score_kernel, chunk=chunk),
        grid=(width // tile,),
        in_specs=[
            pl.BlockSpec((rows, depth), lambda i: (0, 0)),
            pl.BlockSpec((tile, depth), lambda i: (i, 0)),
            pl.BlockSpec((1, tile), lambda i: (0, i)),
            pl.BlockSpec((1, tile), lambda i: (0, i)),
            pl.BlockSpec((rows, LANES), lambda i: (0, 0)),
        ],
        out_specs=[
            pl.BlockSpec((rows, tile), lambda i: (0, i)),
            pl.BlockSpec((1, tile), lambda i: (0, i)),
        ],
        out_shape=[
            jax.ShapeDtypeStruct((rows, width), BF),
            jax.ShapeDtypeStruct((1, width), F32),
        ],
        cost_estimate=pl.CostEstimate(
            flops=2 * rows * width * depth,
            bytes_accessed=2 * (rows * depth + width * depth + rows * width),
            transcendentals=3 * rows * width,
        ),
        name="scores",
    )(x, w, bias, prop, words)


def weight_kernel(*refs):
    out_ref = refs[-1]
    half = (len(refs) - 1) // 2
    total = None
    for x_ref, r_ref in zip(refs[:half], refs[half : 2 * half]):
        term = lax.dot_general(
            x_ref[...], r_ref[...], (((0,), (0,)), ((), ())), preferred_element_type=F32
        )
        total = term if total is None else total + term
    out_ref[...] = total.astype(BF)


def weight_call(xs, rs, tile=512):
    rows, depth = xs[0].shape
    width = rs[0].shape[1]
    return pl.pallas_call(
        weight_kernel,
        grid=(width // tile,),
        in_specs=[pl.BlockSpec((rows, depth), lambda i: (0, 0))] * len(xs)
        + [pl.BlockSpec((rows, tile), lambda i: (0, i))] * len(rs),
        out_specs=pl.BlockSpec((depth, tile), lambda i: (0, i)),
        out_shape=jax.ShapeDtypeStruct((depth, width), BF),
        cost_estimate=pl.CostEstimate(
            flops=2 * len(xs) * rows * width * depth,
            bytes_accessed=2 * (len(xs) * rows * (depth + width) + width * depth),
            transcendentals=0,
        ),
        name="weights",
    )(*xs, *rs)


def sum_over_y(v):
    one, two, three = (lax.ppermute(v, "y", ring(NY, d)) for d in (1, 2, 3))
    return (v + two) + (one + three)


def pair_blocks(terms):
    core, y = lax.axis_index("core"), lax.axis_index("y")
    given = lax.dynamic_index_in_dim(terms, 1 - core, 1, keepdims=False)
    kept = lax.dynamic_index_in_dim(terms, core, 1, keepdims=False)
    pair = kept.astype(F32) + lax.ppermute(given, "core", ring(NC, 1)).astype(F32)
    pair = pair.astype(BF)
    return [lax.dynamic_index_in_dim(pair, (y + d) % NY, 0, keepdims=False) for d in range(NY)]


def bin_prior(bins, prior_mean):
    levels = jnp.arange(prior_mean.shape[0], dtype=jnp.int32)
    onehot = (bins[:, None] == levels[None, :]).astype(F32)
    return jnp.sum(onehot * prior_mean[None, :], axis=1)


def mm(a, b, dims):
    return lax.dot_general(a, b, (dims, ((), ())), preferred_element_type=F32)


def body(
    embeddings, class_weight, class_bias, propensity, label_ids, label_count, label_bins, prior_mean
):
    width, depth = class_weight.shape
    part = embeddings.shape[0]
    block = part * NZ
    x_at = lax.axis_index("x")
    offset = (x_at * NZ + lax.axis_index("z")) * width
    bias, prop = class_bias[None, :], propensity[None, :]

    own = lax.all_to_all(
        jnp.tile(embeddings, (NZ, 1)), "z", split_axis=0, concat_axis=0, tiled=True
    )

    turn = lambda v: lax.dynamic_slice_in_dim(
        jnp.concatenate([v, v], axis=0), x_at * block, v.shape[0], 0
    )
    words = observed_words(turn(label_ids), turn(label_count), offset, width)
    own, words = lax.optimization_barrier((own, words))
    back, far, front = (lax.ppermute(own, "x", ring(NX, -d)) for d in (3, 2, 1))

    def scored(x, first):
        return score_call(x, class_weight, bias, prop, words[first : first + x.shape[0]])

    bits = jnp.arange(width // LANES, dtype=jnp.int32)
    seen = (words[:, None, :] >> bits[None, :, None]) & 1
    obs = jnp.sum(seen.astype(F32), axis=0).reshape(1, width)
    prior = bin_prior(label_bins, prior_mean)

    res0, post0 = scored(own, 0)
    res1, post1 = scored(front, block)
    res3, post3 = scored(back, 3 * block)
    res2, post2 = scored(far, 2 * block)
    post = (post0 + post1) + (post3 + post2)
    sums = jnp.concatenate([obs, post], axis=0)
    sums = sums + lax.ppermute(sums, "core", ring(NC, 1))
    sums, res0 = lax.optimization_barrier((sums, res0))
    sums = sum_over_y(sums)
    updated = ((sums[0:1] + 8.0 * prior[None, :]) / (sums[1:2] + 8.0)).reshape(width)

    weight_terms = weight_call((own, front, back, far), (res0, res1, res3, res2))

    scaled_weight = (class_weight.astype(F32) / updated[:, None]).astype(BF)
    terms = [mm(r, scaled_weight, ((1,), (0,))) for r in (res2, res1, res3, res0)]
    moved = [
        lax.ppermute(t.astype(BF), "x", ring(NX, d)).astype(F32)
        for d, t in zip((2, 1, 3), terms)
    ]
    pairs = pair_blocks(weight_terms.reshape(NY, NC, depth // (NY * NC), width))
    kept, pairs = lax.optimization_barrier((terms[3], pairs))
    weight_sum = pairs[0].astype(F32)
    for d in (1, 2, 3):
        weight_sum = weight_sum + lax.ppermute(pairs[d], "y", ring(NY, d)).astype(F32)
    weight_grad = (weight_sum / updated[None, :]).astype(BF).T

    total = kept + moved[0] + moved[1] + moved[2]
    parts = lax.all_to_all(total.astype(BF), "z", split_axis=0, concat_axis=0, tiled=True)
    embed_grad = jnp.sum(parts.reshape(NZ, part, depth).astype(F32), axis=0).astype(BF)
    return updated, weight_grad, embed_grad


def solution(mesh):
    fine = Mesh(mesh.devices.reshape(NY, NC, NX, NZ), ("y", "core", "x", "z"))
    rows, labels = ("y", "core"), ("x", "z")
    both = rows + labels
    return jax.shard_map(
        body,
        mesh=fine,
        in_specs=(
            P(both, None),
            P(labels, None),
            P(labels),
            P(labels),
            P(rows, None),
            P(rows),
            P(labels),
            P(),
        ),
        out_specs=(P(labels), P(labels, rows), P(both, None)),
        check_vma=False,
    )
```

```python
import functools

import jax
import jax.numpy as jnp
from jax import lax
from jax.experimental import pallas as pl
from jax.experimental.pallas import tpu as pltpu
from jax.sharding import Mesh, PartitionSpec as P

BF = jnp.bfloat16
F32 = jnp.float32
LANES = 128
LOG2E = 1.4426950408889634
NX, NZ, NY, NC = 4, 8, 4, 2


def ring(n, d):
    return [(i, (i + d) % n) for i in range(n)]


def mm(a, b, dims):
    return lax.dot_general(a, b, (dims, ((), ())), preferred_element_type=F32)


def observed_words(label_ids, label_count, offset, width):
    slots = jnp.arange(label_ids.shape[1], dtype=jnp.int32)
    local = label_ids - offset
    valid = (slots[None, :] < label_count[:, None]) & (local >= 0) & (local < width)
    lane = jnp.where(valid, local & (LANES - 1), -1)
    word = jnp.left_shift(jnp.int32(1), jnp.where(valid, local >> 7, 0))
    lanes = jnp.arange(LANES, dtype=jnp.int32)
    hits = jnp.where(lane[:, :, None] == lanes[None, None, :], word[:, :, None], 0)
    return lax.reduce(hits, jnp.int32(0), lax.bitwise_or, (1,))


def score_kernel(*refs, count, chunk, tile):
    x_refs, words_refs = refs[:count], refs[count : 2 * count]
    w_ref, bias_ref, prop_ref = refs[2 * count : 2 * count + 3]
    res_refs, post_ref = refs[2 * count + 3 : -1], refs[-1]
    step = pl.program_id(0)
    cols = pl.ds(pl.multiple_of(step * tile, tile), tile)
    lowest = step * (tile // LANES)
    bias = bias_ref[...] * -LOG2E
    prop = prop_ref[...]
    rest = 1.0 - prop
    total = jnp.zeros((8, tile), F32)
    for x_ref, words_ref, res_ref in zip(x_refs, words_refs, res_refs):
        size = min(chunk, x_ref.shape[0])
        for start in range(0, x_ref.shape[0], size):
            rows = slice(start, start + size)
            scores = mm(x_ref[rows, :], w_ref[cols, :], ((1,), (1,)))
            grown = 1.0 + jnp.exp2(scores * -LOG2E + bias)
            prob = 1.0 / grown
            unseen = rest / (grown - prop)
            words = words_ref[rows, :]
            seen = jnp.concatenate(
                [words & jnp.left_shift(jnp.int32(1), lowest + b) for b in range(tile // LANES)],
                axis=1,
            )
            posterior = jnp.where(seen != 0, 1.0, unseen)
            res_ref[rows, :] = (prob - posterior).astype(BF)
            total = total + jnp.sum(posterior.reshape(size // 8, 8, tile), axis=0)
    post_ref[...] = jnp.sum(total, axis=0, keepdims=True)


def in_vmem(count):
    return [pl.BlockSpec(memory_space=pltpu.VMEM)] * count


def score_call(xs, words, w, bias, prop, chunk=256, tile=512):
    width, depth = w.shape
    rows = sum(x.shape[0] for x in xs)
    narrow = pl.BlockSpec((1, tile), lambda i: (0, i))
    *res, post = pl.pallas_call(
        functools.partial(score_kernel, count=len(xs), chunk=chunk, tile=tile),
        grid=(width // tile,),
        in_specs=in_vmem(2 * len(xs) + 1) + [narrow, narrow],
        out_specs=[pl.BlockSpec((x.shape[0], tile), lambda i: (0, i)) for x in xs] + [narrow],
        out_shape=[pltpu.HBM((x.shape[0], width), BF) for x in xs]
        + [jax.ShapeDtypeStruct((1, width), F32)],
        cost_estimate=pl.CostEstimate(
            flops=2 * rows * width * depth,
            bytes_accessed=2 * (rows * depth + width * depth + rows * width),
            transcendentals=3 * rows * width,
        ),
        compiler_params=pltpu.CompilerParams(vmem_limit_bytes=24 << 20),
        name="scores",
    )(*xs, *words, w, bias, prop)
    return res, post


def weight_kernel(*refs, count):
    x_refs, r_refs = refs[:count], refs[count : 2 * count]
    out_ref, x_all, r_all = refs[2 * count :]

    @pl.when(pl.program_id(0) == 0)
    def _():
        at = 0
        for x_ref in x_refs:
            x_all[at : at + x_ref.shape[0], :] = x_ref[...]
            at += x_ref.shape[0]

    at = 0
    for r_ref in r_refs:
        r_all[at : at + r_ref.shape[0], :] = r_ref[...]
        at += r_ref.shape[0]
    out_ref[...] = mm(x_all[...], r_all[...], ((0,), (0,))).astype(BF)


def weight_call(xs, rs, tile=512):
    depth = xs[0].shape[1]
    width = rs[0].shape[1]
    rows = sum(x.shape[0] for x in xs)
    return pl.pallas_call(
        functools.partial(weight_kernel, count=len(xs)),
        grid=(width // tile,),
        in_specs=[pl.BlockSpec(x.shape, lambda i: (0, 0)) for x in xs]
        + [pl.BlockSpec((r.shape[0], tile), lambda i: (0, i)) for r in rs],
        out_specs=pl.BlockSpec((depth, tile), lambda i: (0, i)),
        out_shape=jax.ShapeDtypeStruct((depth, width), BF),
        scratch_shapes=[pltpu.VMEM((rows, depth), BF), pltpu.VMEM((rows, tile), BF)],
        cost_estimate=pl.CostEstimate(
            flops=2 * rows * width * depth,
            bytes_accessed=2 * (rows * (depth + width) + width * depth),
            transcendentals=0,
        ),
        compiler_params=pltpu.CompilerParams(vmem_limit_bytes=24 << 20),
        name="weights",
    )(*xs, *rs)


def sum_over_y(v):
    one, two, three = (lax.ppermute(v, "y", ring(NY, d)) for d in (1, 2, 3))
    return (v + two) + (one + three)


def pair_blocks(terms):
    core, y = lax.axis_index("core"), lax.axis_index("y")
    given = lax.dynamic_index_in_dim(terms, 1 - core, 1, keepdims=False)
    kept = lax.dynamic_index_in_dim(terms, core, 1, keepdims=False)
    pair = kept.astype(F32) + lax.ppermute(given, "core", ring(NC, 1)).astype(F32)
    pair = pair.astype(BF)
    return [lax.dynamic_index_in_dim(pair, (y + d) % NY, 0, keepdims=False) for d in range(NY)]


def bin_prior(bins, prior_mean):
    levels = jnp.arange(prior_mean.shape[0], dtype=jnp.int32)
    onehot = (bins[:, None] == levels[None, :]).astype(F32)
    return jnp.sum(onehot * prior_mean[None, :], axis=1)


def shift(v, axis, n, d):
    return lax.ppermute(v, axis, ring(n, d))


def exchange(v):
    return lax.all_to_all(v, "z", split_axis=0, concat_axis=0, tiled=True)


def body(
    embeddings, class_weight, class_bias, propensity, label_ids, label_count, label_bins, prior_mean
):
    width, depth = class_weight.shape
    part = embeddings.shape[0]
    cut = 3 * part // 4
    rest = part - cut
    block = part * NZ
    x_at = lax.axis_index("x")
    offset = (x_at * NZ + lax.axis_index("z")) * width
    bias, prop = class_bias[None, :], propensity[None, :]

    piece = embeddings[cut:]
    own = exchange(jnp.tile(embeddings[:cut], (NZ, 1)))
    side = [piece] + [shift(piece, "x", NX, -d) for d in (1, 2, 3)]
    side = jnp.concatenate(side, axis=0)

    turn = lambda v: lax.dynamic_slice_in_dim(
        jnp.concatenate([v, v], axis=0), x_at * block, v.shape[0], 0
    )
    words = observed_words(turn(label_ids), turn(label_count), offset, width)
    own, words = lax.optimization_barrier((own, words))
    fine = words.reshape(NX, NZ, part, LANES)
    near_words = [fine[d, :, :cut].reshape(NZ * cut, LANES) for d in range(NX)]
    side_words = fine[:, :, cut:].transpose(1, 0, 2, 3).reshape(NX * NZ * rest, LANES)
    front, far, back = (shift(own, "x", NX, -d) for d in (1, 2, 3))
    side = exchange(jnp.tile(side, (NZ, 1)))

    bits = jnp.arange(width // LANES, dtype=jnp.int32)
    seen = (words[:, None, :] >> bits[None, :, None]) & 1
    obs = jnp.sum(seen.astype(F32), axis=0).reshape(1, width)
    prior = bin_prior(label_bins, prior_mean)

    (res0,), post0 = score_call((own,), near_words[:1], class_weight, bias, prop)
    (res1, res3), post1 = score_call(
        (front, back), (near_words[1], near_words[3]), class_weight, bias, prop
    )
    (res2, res_side), post2 = score_call(
        (far, side), (near_words[2], side_words), class_weight, bias, prop
    )
    sums = jnp.concatenate([obs, (post0 + post1) + post2], axis=0)
    sums = sums + shift(sums, "core", NC, 1)
    sums = sum_over_y(sums)
    updated = ((sums[0:1] + 8.0 * prior[None, :]) / (sums[1:2] + 8.0)).reshape(width)

    scaled_weight = (class_weight.astype(F32) / updated[:, None]).astype(BF)

    def term(r):
        return mm(r, scaled_weight, ((1,), (0,)))

    side_parts = exchange(term(res_side).astype(BF))
    moved = []
    for d, r in ((2, res2), (1, res1), (3, res3)):
        moved.append(shift(term(r).astype(BF), "x", NX, d).astype(F32))
    kept = term(res0)

    kept, own_rows = lax.optimization_barrier((kept, own))
    weight_terms = weight_call(
        (side, own_rows, front, far, back), (res_side, res0, res1, res2, res3)
    )
    pairs = pair_blocks(weight_terms.reshape(NY, NC, depth // (NY * NC), width))
    kept, pairs = lax.optimization_barrier((kept, pairs))
    weight_sum = pairs[0].astype(F32)
    for d in (1, 2, 3):
        weight_sum = weight_sum + shift(pairs[d], "y", NY, d).astype(F32)
    weight_grad = (weight_sum / updated[None, :]).astype(BF).T

    near = exchange((kept + moved[0] + moved[1] + moved[2]).astype(BF))
    near = jnp.sum(near.reshape(NZ, cut, depth).astype(F32), axis=0).astype(BF)
    side_sum = jnp.sum(side_parts.reshape(NZ, NX, rest, depth).astype(F32), axis=0)
    last = side_sum[0]
    for d in (1, 2, 3):
        last = last + shift(side_sum[d].astype(BF), "x", NX, d).astype(F32)
    return updated, weight_grad, jnp.concatenate([near, last.astype(BF)], axis=0)


def solution(mesh):
    fine = Mesh(mesh.devices.reshape(NY, NC, NX, NZ), ("y", "core", "x", "z"))
    rows, labels = ("y", "core"), ("x", "z")
    both = rows + labels
    return jax.shard_map(
        body,
        mesh=fine,
        in_specs=(
            P(both, None),
            P(labels, None),
            P(labels),
            P(labels),
            P(rows, None),
            P(rows),
            P(labels),
            P(),
        ),
        out_specs=(P(labels), P(labels, rows), P(both, None)),
        check_vma=False,
    )
```

```python
import functools

import jax
import jax.numpy as jnp
from jax import lax
from jax.experimental import pallas as pl
from jax.experimental.pallas import tpu as pltpu
from jax.sharding import Mesh, PartitionSpec as P

BF = jnp.bfloat16
F32 = jnp.float32
LANES = 128
LOG2E = 1.4426950408889634
NX, NZ, NY, NC = 4, 8, 4, 2


def ring(n, d):
    return [(i, (i + d) % n) for i in range(n)]


def mm(a, b, dims):
    return lax.dot_general(a, b, (dims, ((), ())), preferred_element_type=F32)


def words_kernel(at_ref, ids_ref, count_ref, words_ref, obs_ref, *, width):
    slots, rows = ids_ref.shape
    lanes = lax.broadcasted_iota(jnp.int32, (LANES, LANES), 1)
    slot = lax.broadcasted_iota(jnp.int32, (slots, LANES), 0)
    counts = [jnp.zeros((8, LANES), jnp.int32) for _ in range(width // LANES)]
    for first in range(0, rows, LANES):
        turned = lax.rem(at_ref[1] + first, rows)
        source = pl.ds(pl.multiple_of(turned, LANES), LANES)
        local = ids_ref[:, source] - at_ref[0]
        valid = (slot < count_ref[:, source]) & (local >= 0) & (local < width)
        bit = jnp.left_shift(jnp.int32(256), jnp.where(valid, local >> 7, 0))
        code = jnp.where(valid, bit | (local & (LANES - 1)), 255).T
        words = jnp.zeros((LANES, LANES), jnp.int32)
        for i in range(slots):
            here = jnp.broadcast_to(code[:, i : i + 1], (LANES, LANES))
            words = words | jnp.where((here & 255) == lanes, here >> 8, 0)
        words_ref[first : first + LANES, :] = words
        for b in range(width // LANES):
            hit = (words >> b) & 1
            counts[b] = counts[b] + jnp.sum(hit.reshape(LANES // 8, 8, LANES), axis=0)
    for b in range(width // LANES):
        obs_ref[:, b * LANES : (b + 1) * LANES] = jnp.sum(
            counts[b].astype(F32), axis=0, keepdims=True
        )


def words_call(at, ids, count, width):
    rows = ids.shape[1]
    return pl.pallas_call(
        functools.partial(words_kernel, width=width),
        in_specs=[pl.BlockSpec(memory_space=pltpu.SMEM)] + in_vmem(2),
        out_specs=in_vmem(2),
        out_shape=[
            jax.ShapeDtypeStruct((rows, LANES), jnp.int32),
            jax.ShapeDtypeStruct((1, width), F32),
        ],
        cost_estimate=pl.CostEstimate(
            flops=200 * rows * LANES, bytes_accessed=8 * rows * LANES, transcendentals=0
        ),
        compiler_params=pltpu.CompilerParams(vmem_limit_bytes=16 << 20),
        name="words",
    )(at, ids, count)


def score_kernel(*refs, at, chunk, tile):
    count = len(at)
    x_refs, words_ref = refs[:count], refs[count]
    w_ref, bias_ref, prop_ref = refs[count + 1 : count + 4]
    res_refs, post_ref = refs[count + 4 : -1], refs[-1]
    step = pl.program_id(0)
    cols = pl.ds(pl.multiple_of(step * tile, tile), tile)
    lowest = step * (tile // LANES)
    bias = bias_ref[...] * -LOG2E
    prop = prop_ref[...]
    rest = 1.0 - prop
    total = jnp.zeros((8, tile), F32)
    for x_ref, place, res_ref in zip(x_refs, at, res_refs):
        size = min(chunk, x_ref.shape[0])
        for start in range(0, x_ref.shape[0], size):
            rows = slice(start, start + size)
            scores = mm(x_ref[rows, :], w_ref[cols, :], ((1,), (1,)))
            grown = 1.0 + jnp.exp2(scores * -LOG2E + bias)
            prob = 1.0 / grown
            unseen = rest / (grown - prop)
            words = words_ref[place + start : place + start + size, :]
            seen = jnp.concatenate(
                [words & jnp.left_shift(jnp.int32(1), lowest + b) for b in range(tile // LANES)],
                axis=1,
            )
            posterior = jnp.where(seen != 0, 1.0, unseen)
            res_ref[rows, :] = (prob - posterior).astype(BF)
            total = total + jnp.sum(posterior.reshape(size // 8, 8, tile), axis=0)
    post_ref[...] = jnp.sum(total, axis=0, keepdims=True)


def in_vmem(count):
    return [pl.BlockSpec(memory_space=pltpu.VMEM)] * count


def score_call(xs, at, words, w, bias, prop, chunk=256, tile=512):
    width, depth = w.shape
    rows = sum(x.shape[0] for x in xs)
    narrow = pl.BlockSpec((1, tile), lambda i: (0, i))
    *res, post = pl.pallas_call(
        functools.partial(score_kernel, at=at, chunk=chunk, tile=tile),
        grid=(width // tile,),
        in_specs=in_vmem(len(xs) + 2) + [narrow, narrow],
        out_specs=[pl.BlockSpec((x.shape[0], tile), lambda i: (0, i)) for x in xs] + [narrow],
        out_shape=[pltpu.HBM((x.shape[0], width), BF) for x in xs]
        + [jax.ShapeDtypeStruct((1, width), F32)],
        cost_estimate=pl.CostEstimate(
            flops=2 * rows * width * depth,
            bytes_accessed=2 * (rows * depth + width * depth + rows * width),
            transcendentals=3 * rows * width,
        ),
        compiler_params=pltpu.CompilerParams(vmem_limit_bytes=24 << 20),
        name="scores",
    )(*xs, words, w, bias, prop)
    return res, post


def weight_kernel(core_ref, *refs, count):
    x_refs, r_refs = refs[:count], refs[count : 2 * count]
    kept_ref, given_ref, x_all, r_all, out = refs[2 * count :]
    mine = core_ref[0]

    @pl.when(pl.program_id(0) == 0)
    def _():
        at = 0
        for x_ref in x_refs:
            x_all[at : at + x_ref.shape[0], :] = x_ref[...]
            at += x_ref.shape[0]

    at = 0
    for r_ref in r_refs:
        r_all[at : at + r_ref.shape[0], :] = r_ref[...]
        at += r_ref.shape[0]
    out[...] = mm(x_all[...], r_all[...], ((0,), (0,))).astype(BF)
    step = kept_ref.shape[1]
    for y in range(NY):
        kept_ref[y] = out[pl.ds(pl.multiple_of((y * NC + mine) * step, step), step), :]
        given_ref[y] = out[pl.ds(pl.multiple_of((y * NC + 1 - mine) * step, step), step), :]


def weight_call(core, xs, rs, tile=512):
    depth = xs[0].shape[1]
    width = rs[0].shape[1]
    rows = sum(x.shape[0] for x in xs)
    step = depth // (NY * NC)
    half = pl.BlockSpec((NY, step, tile), lambda i: (0, 0, i))
    return pl.pallas_call(
        functools.partial(weight_kernel, count=len(xs)),
        grid=(width // tile,),
        in_specs=[pl.BlockSpec(memory_space=pltpu.SMEM)]
        + [pl.BlockSpec(x.shape, lambda i: (0, 0)) for x in xs]
        + [pl.BlockSpec((r.shape[0], tile), lambda i: (0, i)) for r in rs],
        out_specs=[half, half],
        out_shape=[pltpu.HBM((NY, step, width), BF)] * 2,
        scratch_shapes=[
            pltpu.VMEM((rows, depth), BF),
            pltpu.VMEM((rows, tile), BF),
            pltpu.VMEM((depth, tile), BF),
        ],
        cost_estimate=pl.CostEstimate(
            flops=2 * rows * width * depth,
            bytes_accessed=2 * (rows * (depth + width) + width * depth),
            transcendentals=0,
        ),
        compiler_params=pltpu.CompilerParams(vmem_limit_bytes=60 << 20),
        name="weights",
    )(core, *xs, *rs)


def bin_prior(bins, prior_mean):
    levels = jnp.arange(prior_mean.shape[0], dtype=jnp.int32)
    onehot = (bins[:, None] == levels[None, :]).astype(F32)
    return jnp.sum(onehot * prior_mean[None, :], axis=1)


def shift(v, axis, n, d):
    return lax.ppermute(v, axis, ring(n, d))


def exchange(v, axis):
    return lax.all_to_all(v, axis, split_axis=0, concat_axis=0, tiled=True)


def body(
    embeddings, class_weight, class_bias, propensity, label_ids, label_count, label_bins, prior_mean
):
    width, depth = class_weight.shape
    part = embeddings.shape[0]
    block = part * NZ
    x_at, core, y = (lax.axis_index(a) for a in ("x", "core", "y"))
    offset = (x_at * NZ + lax.axis_index("z")) * width
    bias, prop = class_bias[None, :], propensity[None, :]

    own = exchange(jnp.tile(embeddings, (NZ, 1)), "z")
    at = jnp.stack([offset, x_at * block])
    words, obs = words_call(at, label_ids.T, label_count[None, :], width)
    prior = bin_prior(label_bins, prior_mean)

    def brought(d):
        return shift(own, "x", NX, -d)

    front, back, far = brought(1), brought(3), brought(2)
    (res0,), post0 = score_call((own,), (0,), words, class_weight, bias, prop)
    (res1,), post1 = score_call((front,), (block,), words, class_weight, bias, prop)
    (res3,), post3 = score_call((back,), (3 * block,), words, class_weight, bias, prop)
    (res2,), post2 = score_call((far,), (2 * block,), words, class_weight, bias, prop)
    post = (post0 + post1) + (post3 + post2)
    both = jnp.concatenate([obs, post], axis=0)[None]
    sums = jnp.sum(exchange(jnp.tile(both, (NY * NC, 1, 1)), ("y", "core")), axis=0)
    updated = ((sums[0:1] + 8.0 * prior[None, :]) / (sums[1:2] + 8.0)).reshape(width)

    kept_rows, given = weight_call(core[None], (own, front, far, back), (res0, res1, res2, res3))
    pair = kept_rows.astype(F32) + shift(given, "core", NC, 1).astype(F32)
    pair = pair.astype(BF)
    pairs = [lax.dynamic_index_in_dim(pair, (y + d) % NY, 0, keepdims=False) for d in range(NY)]

    scaled_weight = (class_weight.astype(F32) / updated[:, None]).astype(BF)

    def term(r):
        return mm(r, scaled_weight, ((1,), (0,)))

    moved = []
    for d, r in ((2, res2), (1, res1), (3, res3)):
        moved.append(shift(term(r).astype(BF), "x", NX, d).astype(F32))
    kept = term(res0)
    kept, pairs = lax.optimization_barrier((kept, pairs))
    weight_sum = pairs[0].astype(F32)
    for d in (1, 2, 3):
        weight_sum = weight_sum + shift(pairs[d], "y", NY, d).astype(F32)
    weight_grad = (weight_sum / updated[None, :]).astype(BF).T

    parts = exchange((kept + moved[0] + moved[1] + moved[2]).astype(BF), "z")
    embed_grad = jnp.sum(parts.reshape(NZ, part, depth).astype(F32), axis=0).astype(BF)
    return updated, weight_grad, embed_grad


def solution(mesh):
    fine = Mesh(mesh.devices.reshape(NY, NC, NX, NZ), ("y", "core", "x", "z"))
    rows, labels = ("y", "core"), ("x", "z")
    both = rows + labels
    return jax.shard_map(
        body,
        mesh=fine,
        in_specs=(
            P(both, None),
            P(labels, None),
            P(labels),
            P(labels),
            P(rows, None),
            P(rows),
            P(labels),
            P(),
        ),
        out_specs=(P(labels), P(labels, rows), P(both, None)),
        check_vma=False,
    )
```

```python
import functools

import jax
import jax.numpy as jnp
from jax import lax
from jax.experimental import pallas as pl
from jax.experimental.pallas import tpu as pltpu
from jax.sharding import Mesh, PartitionSpec as P

BF = jnp.bfloat16
F32 = jnp.float32
LANES = 128
LOG2E = 1.4426950408889634
NX, NZ, NY, NC = 4, 8, 4, 2


def ring(n, d):
    return [(i, (i + d) % n) for i in range(n)]


def mm(a, b, dims):
    return lax.dot_general(a, b, (dims, ((), ())), preferred_element_type=F32)


def words_kernel(at_ref, ids_ref, count_ref, words_ref, obs_ref, *, width):
    slots, rows = ids_ref.shape
    lanes = lax.broadcasted_iota(jnp.int32, (LANES, LANES), 1)
    slot = lax.broadcasted_iota(jnp.int32, (slots, LANES), 0)
    counts = [jnp.zeros((8, LANES), jnp.int32) for _ in range(width // LANES)]
    for first in range(0, rows, LANES):
        turned = lax.rem(at_ref[1] + first, rows)
        source = pl.ds(pl.multiple_of(turned, LANES), LANES)
        local = ids_ref[:, source] - at_ref[0]
        valid = (slot < count_ref[:, source]) & (local >= 0) & (local < width)
        bit = jnp.left_shift(jnp.int32(256), jnp.where(valid, local >> 7, 0))
        code = jnp.where(valid, bit | (local & (LANES - 1)), 255).T
        words = jnp.zeros((LANES, LANES), jnp.int32)
        for i in range(slots):
            here = jnp.broadcast_to(code[:, i : i + 1], (LANES, LANES))
            words = words | jnp.where((here & 255) == lanes, here >> 8, 0)
        words_ref[first : first + LANES, :] = words
        for b in range(width // LANES):
            hit = (words >> b) & 1
            counts[b] = counts[b] + jnp.sum(hit.reshape(LANES // 8, 8, LANES), axis=0)
    for b in range(width // LANES):
        obs_ref[:, b * LANES : (b + 1) * LANES] = jnp.sum(
            counts[b].astype(F32), axis=0, keepdims=True
        )


def words_call(at, ids, count, width):
    rows = ids.shape[1]
    return pl.pallas_call(
        functools.partial(words_kernel, width=width),
        in_specs=[pl.BlockSpec(memory_space=pltpu.SMEM)] + in_vmem(2),
        out_specs=in_vmem(2),
        out_shape=[
            jax.ShapeDtypeStruct((rows, LANES), jnp.int32),
            jax.ShapeDtypeStruct((1, width), F32),
        ],
        cost_estimate=pl.CostEstimate(
            flops=200 * rows * LANES, bytes_accessed=8 * rows * LANES, transcendentals=0
        ),
        compiler_params=pltpu.CompilerParams(vmem_limit_bytes=16 << 20),
        name="words",
    )(at, ids, count)


def score_kernel(*refs, at, chunk, tile):
    count = len(at)
    x_refs, words_ref = refs[:count], refs[count]
    w_ref, bias_ref, prop_ref = refs[count + 1 : count + 4]
    res_refs, post_ref = refs[count + 4 : 2 * count + 4], refs[2 * count + 4]
    slots, sems = refs[2 * count + 5 : 3 * count + 5], refs[3 * count + 5]
    copies = []
    for t in range(w_ref.shape[0] // tile):
        cols = slice(t * tile, (t + 1) * tile)
        bias = bias_ref[:, cols] * -LOG2E
        prop = prop_ref[:, cols]
        rest = 1.0 - prop
        total = jnp.zeros((8, tile), F32)
        for k in range(count):
            size = min(chunk, x_refs[k].shape[0])
            for start in range(0, x_refs[k].shape[0], size):
                rows = slice(start, start + size)
                scores = mm(x_refs[k][rows, :], w_ref[cols, :], ((1,), (1,)))
                grown = 1.0 + jnp.exp2(scores * -LOG2E + bias)
                prob = 1.0 / grown
                unseen = rest / (grown - prop)
                words = words_ref[at[k] + start : at[k] + start + size, :]
                bits = range(t * tile // LANES, (t + 1) * tile // LANES)
                seen = jnp.concatenate([words & (1 << b) for b in bits], axis=1)
                posterior = jnp.where(seen != 0, 1.0, unseen)
                slots[k][t, rows, :] = (prob - posterior).astype(BF)
                total = total + jnp.sum(posterior.reshape(size // 8, 8, tile), axis=0)
            copy = pltpu.make_async_copy(slots[k].at[t], res_refs[k].at[:, cols], sems.at[k, t])
            copy.start()
            copies.append(copy)
        post_ref[:, cols] = jnp.sum(total, axis=0, keepdims=True)
    for copy in copies:
        copy.wait()


def in_vmem(count):
    return [pl.BlockSpec(memory_space=pltpu.VMEM)] * count


def score_call(xs, at, words, w, bias, prop, chunk=256, tile=512):
    width, depth = w.shape
    rows = sum(x.shape[0] for x in xs)
    tiles = width // tile
    *res, post = pl.pallas_call(
        functools.partial(score_kernel, at=at, chunk=chunk, tile=tile),
        in_specs=in_vmem(len(xs) + 4),
        out_specs=[pl.BlockSpec(memory_space=pltpu.HBM)] * len(xs) + in_vmem(1),
        out_shape=[pltpu.HBM((x.shape[0], width), BF) for x in xs]
        + [jax.ShapeDtypeStruct((1, width), F32)],
        scratch_shapes=[pltpu.VMEM((tiles, x.shape[0], tile), BF) for x in xs]
        + [pltpu.SemaphoreType.DMA((len(xs), tiles))],
        cost_estimate=pl.CostEstimate(
            flops=2 * rows * width * depth,
            bytes_accessed=2 * (rows * depth + width * depth + rows * width),
            transcendentals=3 * rows * width,
        ),
        compiler_params=pltpu.CompilerParams(vmem_limit_bytes=24 << 20),
        name="scores",
    )(*xs, words, w, bias, prop)
    return res, post


def weight_kernel(core_ref, *refs, count):
    x_refs, r_refs = refs[:count], refs[count : 2 * count]
    kept_ref, given_ref, x_all, r_all, out = refs[2 * count :]
    mine = core_ref[0]

    @pl.when(pl.program_id(0) == 0)
    def _():
        at = 0
        for x_ref in x_refs:
            x_all[at : at + x_ref.shape[0], :] = x_ref[...]
            at += x_ref.shape[0]

    at = 0
    for r_ref in r_refs:
        r_all[at : at + r_ref.shape[0], :] = r_ref[...]
        at += r_ref.shape[0]
    out[...] = mm(x_all[...], r_all[...], ((0,), (0,))).astype(BF)
    step = kept_ref.shape[1]
    for y in range(NY):
        kept_ref[y] = out[pl.ds(pl.multiple_of((y * NC + mine) * step, step), step), :]
        given_ref[y] = out[pl.ds(pl.multiple_of((y * NC + 1 - mine) * step, step), step), :]


def weight_call(core, xs, rs, tile=512):
    depth = xs[0].shape[1]
    width = rs[0].shape[1]
    rows = sum(x.shape[0] for x in xs)
    step = depth // (NY * NC)
    half = pl.BlockSpec((NY, step, tile), lambda i: (0, 0, i))
    return pl.pallas_call(
        functools.partial(weight_kernel, count=len(xs)),
        grid=(width // tile,),
        in_specs=[pl.BlockSpec(memory_space=pltpu.SMEM)]
        + [pl.BlockSpec(x.shape, lambda i: (0, 0)) for x in xs]
        + [pl.BlockSpec((r.shape[0], tile), lambda i: (0, i)) for r in rs],
        out_specs=[half, half],
        out_shape=[pltpu.HBM((NY, step, width), BF)] * 2,
        scratch_shapes=[
            pltpu.VMEM((rows, depth), BF),
            pltpu.VMEM((rows, tile), BF),
            pltpu.VMEM((depth, tile), BF),
        ],
        cost_estimate=pl.CostEstimate(
            flops=2 * rows * width * depth,
            bytes_accessed=2 * (rows * (depth + width) + width * depth),
            transcendentals=0,
        ),
        compiler_params=pltpu.CompilerParams(vmem_limit_bytes=60 << 20),
        name="weights",
    )(core, *xs, *rs)


def bin_prior(bins, prior_mean):
    levels = jnp.arange(prior_mean.shape[0], dtype=jnp.int32)
    onehot = (bins[:, None] == levels[None, :]).astype(F32)
    return jnp.sum(onehot * prior_mean[None, :], axis=1)


def shift(v, axis, n, d):
    return lax.ppermute(v, axis, ring(n, d))


def exchange(v, axis):
    return lax.all_to_all(v, axis, split_axis=0, concat_axis=0, tiled=True)


def body(
    embeddings, class_weight, class_bias, propensity, label_ids, label_count, label_bins, prior_mean
):
    width, depth = class_weight.shape
    part = embeddings.shape[0]
    block = part * NZ
    x_at, core, y = (lax.axis_index(a) for a in ("x", "core", "y"))
    offset = (x_at * NZ + lax.axis_index("z")) * width
    bias, prop = class_bias[None, :], propensity[None, :]

    own = exchange(jnp.tile(embeddings, (NZ, 1)), "z")
    at = jnp.stack([offset, x_at * block])
    words, obs = words_call(at, label_ids.T, label_count[None, :], width)
    prior = bin_prior(label_bins, prior_mean)

    def brought(d):
        return shift(own, "x", NX, -d)

    front, back, far = brought(1), brought(3), brought(2)
    (res0,), post0 = score_call((own,), (0,), words, class_weight, bias, prop)
    (res1, res3), post1 = score_call(
        (front, back), (block, 3 * block), words, class_weight, bias, prop
    )
    far, post1 = lax.optimization_barrier((far, post1))
    (res2,), post2 = score_call((far,), (2 * block,), words, class_weight, bias, prop)
    post = (post0 + post1) + post2
    both = jnp.concatenate([obs, post], axis=0)[None]
    sums = jnp.sum(exchange(jnp.tile(both, (NY * NC, 1, 1)), ("y", "core")), axis=0)
    updated = ((sums[0:1] + 8.0 * prior[None, :]) / (sums[1:2] + 8.0)).reshape(width)

    kept_rows, given = weight_call(core[None], (own, front, far, back), (res0, res1, res2, res3))
    pair = kept_rows.astype(F32) + shift(given, "core", NC, 1).astype(F32)
    pair = pair.astype(BF)
    pairs = [lax.dynamic_index_in_dim(pair, (y + d) % NY, 0, keepdims=False) for d in range(NY)]

    scaled_weight = (class_weight.astype(F32) / updated[:, None]).astype(BF)

    def term(r):
        return mm(r, scaled_weight, ((1,), (0,)))

    moved = []
    for d, r in ((2, res2), (1, res1), (3, res3)):
        moved.append(shift(term(r).astype(BF), "x", NX, d).astype(F32))
    kept = term(res0)
    kept, pairs = lax.optimization_barrier((kept, pairs))
    weight_sum = pairs[0].astype(F32)
    for d in (1, 2, 3):
        weight_sum = weight_sum + shift(pairs[d], "y", NY, d).astype(F32)
    weight_grad = (weight_sum / updated[None, :]).astype(BF).T

    parts = exchange((kept + moved[0] + moved[1] + moved[2]).astype(BF), "z")
    embed_grad = jnp.sum(parts.reshape(NZ, part, depth).astype(F32), axis=0).astype(BF)
    return updated, weight_grad, embed_grad


def solution(mesh):
    fine = Mesh(mesh.devices.reshape(NY, NC, NX, NZ), ("y", "core", "x", "z"))
    rows, labels = ("y", "core"), ("x", "z")
    both = rows + labels
    return jax.shard_map(
        body,
        mesh=fine,
        in_specs=(
            P(both, None),
            P(labels, None),
            P(labels),
            P(labels),
            P(rows, None),
            P(rows),
            P(labels),
            P(),
        ),
        out_specs=(P(labels), P(labels, rows), P(both, None)),
        check_vma=False,
    )
```

```python
import functools

import jax
import jax.numpy as jnp
from jax import lax
from jax.experimental import pallas as pl
from jax.experimental.pallas import tpu as pltpu
from jax.sharding import Mesh, PartitionSpec as P

BF = jnp.bfloat16
F32 = jnp.float32
LANES = 128
LOG2E = 1.4426950408889634
NX, NZ, NY, NC = 4, 8, 4, 2


def ring(n, d):
    return [(i, (i + d) % n) for i in range(n)]


def mm(a, b, dims):
    return lax.dot_general(a, b, (dims, ((), ())), preferred_element_type=F32)


def words_kernel(at_ref, ids_ref, count_ref, words_ref, obs_ref, *, width):
    slots, rows = ids_ref.shape
    lanes = lax.broadcasted_iota(jnp.int32, (LANES, LANES), 1)
    slot = lax.broadcasted_iota(jnp.int32, (slots, LANES), 0)
    counts = [jnp.zeros((8, LANES), jnp.int32) for _ in range(width // LANES)]
    for first in range(0, rows, LANES):
        turned = lax.rem(at_ref[1] + first, rows)
        source = pl.ds(pl.multiple_of(turned, LANES), LANES)
        local = ids_ref[:, source] - at_ref[0]
        valid = (slot < count_ref[:, source]) & (local >= 0) & (local < width)
        bit = jnp.left_shift(jnp.int32(256), jnp.where(valid, local >> 7, 0))
        code = jnp.where(valid, bit | (local & (LANES - 1)), 255).T
        words = jnp.zeros((LANES, LANES), jnp.int32)
        for i in range(slots):
            here = jnp.broadcast_to(code[:, i : i + 1], (LANES, LANES))
            words = words | jnp.where((here & 255) == lanes, here >> 8, 0)
        words_ref[first : first + LANES, :] = words
        for b in range(width // LANES):
            hit = (words >> b) & 1
            counts[b] = counts[b] + jnp.sum(hit.reshape(LANES // 8, 8, LANES), axis=0)
    for b in range(width // LANES):
        obs_ref[:, b * LANES : (b + 1) * LANES] = jnp.sum(
            counts[b].astype(F32), axis=0, keepdims=True
        )


def words_call(at, ids, count, width):
    rows = ids.shape[1]
    return pl.pallas_call(
        functools.partial(words_kernel, width=width),
        in_specs=[pl.BlockSpec(memory_space=pltpu.SMEM)] + in_vmem(2),
        out_specs=in_vmem(2),
        out_shape=[
            jax.ShapeDtypeStruct((rows, LANES), jnp.int32),
            jax.ShapeDtypeStruct((1, width), F32),
        ],
        cost_estimate=pl.CostEstimate(
            flops=200 * rows * LANES, bytes_accessed=8 * rows * LANES, transcendentals=0
        ),
        compiler_params=pltpu.CompilerParams(vmem_limit_bytes=16 << 20),
        name="words",
    )(at, ids, count)


def score_kernel(*refs, at, parts, tile):
    count = len(at)
    x_refs, refs = refs[: sum(parts)], refs[sum(parts) :]
    words_ref, w_ref, bias_ref, prop_ref = refs[:4]
    res_refs, post_ref = refs[4 : count + 4], refs[count + 4]
    slots, sems = refs[count + 5 : 2 * count + 5], refs[2 * count + 5]
    starts = [sum(parts[:k]) for k in range(count)]
    blocks = [x_refs[s : s + p] for s, p in zip(starts, parts)]
    copies = []
    for t in range(w_ref.shape[0] // tile):
        cols = slice(t * tile, (t + 1) * tile)
        bias = bias_ref[:, cols] * -LOG2E
        prop = prop_ref[:, cols]
        rest = 1.0 - prop
        total = jnp.zeros((8, tile), F32)
        for k in range(count):
            x = jnp.concatenate([x_ref[...] for x_ref in blocks[k]], axis=0)
            size = x.shape[0]
            scores = mm(x, w_ref[cols, :], ((1,), (1,)))
            grown = 1.0 + jnp.exp2(scores * -LOG2E + bias)
            prob = 1.0 / grown
            unseen = rest / (grown - prop)
            words = words_ref[at[k] : at[k] + size, :]
            bits = range(t * tile // LANES, (t + 1) * tile // LANES)
            seen = jnp.concatenate([words & (1 << b) for b in bits], axis=1)
            posterior = jnp.where(seen != 0, 1.0, unseen)
            slots[k][t] = (prob - posterior).astype(BF)
            total = total + jnp.sum(posterior.reshape(size // 8, 8, tile), axis=0)
            copy = pltpu.make_async_copy(slots[k].at[t], res_refs[k].at[:, cols], sems.at[k, t])
            copy.start()
            copies.append(copy)
        post_ref[:, cols] = jnp.sum(total, axis=0, keepdims=True)
    for copy in copies:
        copy.wait()


def in_vmem(count):
    return [pl.BlockSpec(memory_space=pltpu.VMEM)] * count


def score_call(groups, at, words, w, bias, prop, tile=512):
    width, depth = w.shape
    xs = [x for group in groups for x in group]
    sizes = [sum(x.shape[0] for x in group) for group in groups]
    rows = sum(sizes)
    tiles = width // tile
    parts = tuple(len(group) for group in groups)
    *res, post = pl.pallas_call(
        functools.partial(score_kernel, at=at, parts=parts, tile=tile),
        in_specs=in_vmem(len(xs) + 4),
        out_specs=[pl.BlockSpec(memory_space=pltpu.HBM)] * len(sizes) + in_vmem(1),
        out_shape=[pltpu.HBM((size, width), BF) for size in sizes]
        + [jax.ShapeDtypeStruct((1, width), F32)],
        scratch_shapes=[pltpu.VMEM((tiles, size, tile), BF) for size in sizes]
        + [pltpu.SemaphoreType.DMA((len(sizes), tiles))],
        cost_estimate=pl.CostEstimate(
            flops=2 * rows * width * depth,
            bytes_accessed=2 * (rows * depth + width * depth + rows * width),
            transcendentals=3 * rows * width,
        ),
        compiler_params=pltpu.CompilerParams(vmem_limit_bytes=24 << 20),
        name="scores",
    )(*xs, words, w, bias, prop)
    return res, post


def weight_kernel(core_ref, *refs, count):
    x_refs, r_refs = refs[:count], refs[count:-5]
    kept_ref, given_ref, x_all, r_all, out = refs[-5:]
    mine = core_ref[0]

    @pl.when(pl.program_id(0) == 0)
    def _():
        at = 0
        for x_ref in x_refs:
            x_all[at : at + x_ref.shape[0], :] = x_ref[...]
            at += x_ref.shape[0]

    at = 0
    for r_ref in r_refs:
        r_all[at : at + r_ref.shape[0], :] = r_ref[...]
        at += r_ref.shape[0]
    out[...] = mm(x_all[...], r_all[...], ((0,), (0,))).astype(BF)
    step = kept_ref.shape[1]
    for y in range(NY):
        kept_ref[y] = out[pl.ds(pl.multiple_of((y * NC + mine) * step, step), step), :]
        given_ref[y] = out[pl.ds(pl.multiple_of((y * NC + 1 - mine) * step, step), step), :]


def weight_call(core, xs, rs, tile=512):
    depth = xs[0].shape[1]
    width = rs[0].shape[1]
    rows = sum(x.shape[0] for x in xs)
    step = depth // (NY * NC)
    half = pl.BlockSpec((NY, step, tile), lambda i: (0, 0, i))
    return pl.pallas_call(
        functools.partial(weight_kernel, count=len(xs)),
        grid=(width // tile,),
        in_specs=[pl.BlockSpec(memory_space=pltpu.SMEM)]
        + [pl.BlockSpec(x.shape, lambda i: (0, 0)) for x in xs]
        + [pl.BlockSpec((r.shape[0], tile), lambda i: (0, i)) for r in rs],
        out_specs=[half, half],
        out_shape=[pltpu.HBM((NY, step, width), BF)] * 2,
        scratch_shapes=[
            pltpu.VMEM((rows, depth), BF),
            pltpu.VMEM((rows, tile), BF),
            pltpu.VMEM((depth, tile), BF),
        ],
        cost_estimate=pl.CostEstimate(
            flops=2 * rows * width * depth,
            bytes_accessed=2 * (rows * (depth + width) + width * depth),
            transcendentals=0,
        ),
        compiler_params=pltpu.CompilerParams(vmem_limit_bytes=60 << 20),
        name="weights",
    )(core, *xs, *rs)


def bin_prior(bins, prior_mean):
    levels = jnp.arange(prior_mean.shape[0], dtype=jnp.int32)
    onehot = (bins[:, None] == levels[None, :]).astype(F32)
    return jnp.sum(onehot * prior_mean[None, :], axis=1)


def shift(v, axis, n, d):
    return lax.ppermute(v, axis, ring(n, d))


def exchange(v, axis):
    return lax.all_to_all(v, axis, split_axis=0, concat_axis=0, tiled=True)


def body(
    embeddings, class_weight, class_bias, propensity, label_ids, label_count, label_bins, prior_mean
):
    width, depth = class_weight.shape
    part = embeddings.shape[0]
    block = part * NZ
    x_at, core, y = (lax.axis_index(a) for a in ("x", "core", "y"))
    offset = (x_at * NZ + lax.axis_index("z")) * width
    bias, prop = class_bias[None, :], propensity[None, :]

    own = exchange(jnp.tile(embeddings, (NZ, 1)), "z")
    at = jnp.stack([offset, x_at * block])
    words, obs = words_call(at, label_ids.T, label_count[None, :], width)
    prior = bin_prior(label_bins, prior_mean)

    half = block // 2
    front, back = shift(own, "x", NX, -1), shift(own, "x", NX, 1)
    far = (shift(front[:half], "x", NX, -1), shift(back[half:], "x", NX, 1))
    (res0,), post0 = score_call(((own,),), (0,), words, class_weight, bias, prop)
    (res1, res3), post1 = score_call(
        ((front,), (back,)), (block, 3 * block), words, class_weight, bias, prop
    )
    far, post1 = lax.optimization_barrier((far, post1))
    (res2,), post2 = score_call((far,), (2 * block,), words, class_weight, bias, prop)
    post = (post0 + post1) + post2
    both = jnp.concatenate([obs, post], axis=0)[None]
    sums = jnp.sum(exchange(jnp.tile(both, (NY * NC, 1, 1)), ("y", "core")), axis=0)
    updated = ((sums[0:1] + 8.0 * prior[None, :]) / (sums[1:2] + 8.0)).reshape(width)

    kept_rows, given = weight_call(core[None], (own, front, *far, back), (res0, res1, res2, res3))
    pair = kept_rows.astype(F32) + shift(given, "core", NC, 1).astype(F32)
    pair = pair.astype(BF)
    pairs = [lax.dynamic_index_in_dim(pair, (y + d) % NY, 0, keepdims=False) for d in range(NY)]

    scaled_weight = (class_weight.astype(F32) / updated[:, None]).astype(BF)

    def term(r):
        return mm(r, scaled_weight, ((1,), (0,)))

    send = lambda v, d: shift(v.astype(BF), "x", NX, d).astype(F32)
    term2 = term(res2).astype(BF)
    low2, high2 = send(term2[:half], 1), send(term2[half:], -1)
    term1 = lax.optimization_barrier(term(res1))
    term3 = lax.optimization_barrier(term(res3))
    high1, low3 = send(term1[half:], 1), send(term3[:half], -1)
    kept = term(res0)
    low1, high3 = send(term1[:half] + low2, 1), send(term3[half:] + high2, -1)
    kept, pairs = lax.optimization_barrier((kept, pairs))
    weight_sum = pairs[0].astype(F32)
    for d in (1, 2, 3):
        weight_sum = weight_sum + shift(pairs[d], "y", NY, d).astype(F32)
    weight_grad = (weight_sum / updated[None, :]).astype(BF).T

    low, high = kept[:half] + low1 + low3, kept[half:] + high1 + high3
    parts = exchange(jnp.concatenate([low, high], axis=0).astype(BF), "z")
    embed_grad = jnp.sum(parts.reshape(NZ, part, depth).astype(F32), axis=0).astype(BF)
    return updated, weight_grad, embed_grad


def solution(mesh):
    fine = Mesh(mesh.devices.reshape(NY, NC, NX, NZ), ("y", "core", "x", "z"))
    rows, labels = ("y", "core"), ("x", "z")
    both = rows + labels
    return jax.shard_map(
        body,
        mesh=fine,
        in_specs=(
            P(both, None),
            P(labels, None),
            P(labels),
            P(labels),
            P(rows, None),
            P(rows),
            P(labels),
            P(),
        ),
        out_specs=(P(labels), P(labels, rows), P(both, None)),
        check_vma=False,
    )
```

```python
import functools

import jax
import jax.numpy as jnp
from jax import lax
from jax.experimental import pallas as pl
from jax.experimental.pallas import tpu as pltpu
from jax.sharding import Mesh, PartitionSpec as P

BF = jnp.bfloat16
F32 = jnp.float32
LANES = 128
LOG2E = 1.4426950408889634
NX, NZ, NY, NC = 4, 8, 4, 2


def ring(n, d):
    return [(i, (i + d) % n) for i in range(n)]


def mm(a, b, dims):
    return lax.dot_general(a, b, (dims, ((), ())), preferred_element_type=F32)


def words_kernel(
    at_ref, mean_ref, ids_ref, count_ref, bias_ref, prop_ref, bins_ref, words_ref, obs_ref, label_ref
):
    slots, rows = ids_ref.shape
    width = bias_ref.shape[1]
    label_ref[0:1, :] = bias_ref[...] * -LOG2E
    label_ref[1:2, :] = prop_ref[...]
    bins = bins_ref[...]
    prior = jnp.zeros((1, width), F32)
    for b in range(mean_ref.shape[0]):
        prior = prior + jnp.where(bins == b, mean_ref[b], 0.0)
    label_ref[2:3, :] = 8.0 * prior
    lanes = lax.broadcasted_iota(jnp.int32, (LANES, LANES), 1)
    slot = lax.broadcasted_iota(jnp.int32, (slots, LANES), 0)
    counts = [jnp.zeros((8, LANES), jnp.int32) for _ in range(width // LANES)]
    for first in range(0, rows, LANES):
        turned = lax.rem(at_ref[1] + first, rows)
        source = pl.ds(pl.multiple_of(turned, LANES), LANES)
        local = ids_ref[:, source] - at_ref[0]
        valid = (slot < count_ref[:, source]) & (local >= 0) & (local < width)
        bit = jnp.left_shift(jnp.int32(256), jnp.where(valid, local >> 7, 0))
        code = jnp.where(valid, bit | (local & (LANES - 1)), 255).T
        words = jnp.zeros((LANES, LANES), jnp.int32)
        for i in range(slots):
            here = jnp.broadcast_to(code[:, i : i + 1], (LANES, LANES))
            words = words | jnp.where((here & 255) == lanes, here >> 8, 0)
        words_ref[first : first + LANES, :] = words
        for b in range(width // LANES):
            hit = (words >> b) & 1
            counts[b] = counts[b] + jnp.sum(hit.reshape(LANES // 8, 8, LANES), axis=0)
    for b in range(width // LANES):
        obs_ref[:, b * LANES : (b + 1) * LANES] = jnp.sum(
            counts[b].astype(F32), axis=0, keepdims=True
        )


def words_call(at, mean, ids, count, bias, prop, bins):
    rows, width = ids.shape[1], bias.shape[1]
    return pl.pallas_call(
        words_kernel,
        in_specs=[pl.BlockSpec(memory_space=pltpu.SMEM)] * 2 + in_vmem(5),
        out_specs=in_vmem(3),
        out_shape=[
            jax.ShapeDtypeStruct((rows, LANES), jnp.int32),
            jax.ShapeDtypeStruct((1, width), F32),
            jax.ShapeDtypeStruct((3, width), F32),
        ],
        cost_estimate=pl.CostEstimate(
            flops=200 * rows * LANES, bytes_accessed=8 * rows * LANES, transcendentals=0
        ),
        compiler_params=pltpu.CompilerParams(vmem_limit_bytes=16 << 20),
        name="words",
    )(at, mean, ids, count, bias, prop, bins)


def score_kernel(*refs, at, parts, sizes, tile):
    count = len(at)
    x_refs, refs = refs[: sum(parts)], refs[sum(parts) :]
    words_ref, w_ref, label_ref = refs[:3]
    res_refs, post_ref, refs = refs[3 : count + 3], refs[count + 3], refs[count + 4 :]
    x_in, words_in, slots = refs[:count], refs[count : 2 * count], refs[2 * count : 3 * count]
    w_in, label_in, x_sems, words_sems, w_sems, label_sem, out_sems = refs[3 * count :]
    tiles = w_ref.shape[0] // tile

    first = []
    n = 0
    for k in range(count):
        low = 0
        for _ in range(parts[k]):
            size = x_refs[n].shape[0]
            target = x_in[k].at[low : low + size, :]
            first.append(pltpu.make_async_copy(x_refs[n], target, x_sems.at[n]))
            low, n = low + size, n + 1
        source = words_ref.at[at[k] : at[k] + sizes[k], :]
        first.append(pltpu.make_async_copy(source, words_in[k], words_sems.at[k]))
    first.append(pltpu.make_async_copy(label_ref, label_in, label_sem))
    weights = [
        pltpu.make_async_copy(w_ref.at[t * tile : (t + 1) * tile, :], w_in.at[t], w_sems.at[t])
        for t in range(tiles)
    ]
    for copy in first + weights:
        copy.start()
    for copy in first:
        copy.wait()

    outs = []
    for t in range(tiles):
        weights[t].wait()
        cols = slice(t * tile, (t + 1) * tile)
        bias, prop = label_in[0:1, cols], label_in[1:2, cols]
        rest = 1.0 - prop
        total = jnp.zeros((8, tile), F32)
        for k in range(count):
            size = sizes[k]
            scores = mm(x_in[k][...], w_in[t], ((1,), (1,)))
            grown = 1.0 + jnp.exp2(scores * -LOG2E + bias)
            prob = 1.0 / grown
            unseen = rest / (grown - prop)
            words = words_in[k][...]
            bits = range(t * tile // LANES, (t + 1) * tile // LANES)
            seen = jnp.concatenate([words & (1 << b) for b in bits], axis=1)
            posterior = jnp.where(seen != 0, 1.0, unseen)
            slots[k][t] = (prob - posterior).astype(BF)
            total = total + jnp.sum(posterior.reshape(size // 8, 8, tile), axis=0)
            copy = pltpu.make_async_copy(
                slots[k].at[t], res_refs[k].at[:, cols], out_sems.at[k, t]
            )
            copy.start()
            outs.append(copy)
        post_ref[:, cols] = jnp.sum(total, axis=0, keepdims=True)
    for copy in outs:
        copy.wait()


def in_vmem(count):
    return [pl.BlockSpec(memory_space=pltpu.VMEM)] * count


def score_call(groups, at, words, w, label, tile=512):
    width, depth = w.shape
    xs = [x for group in groups for x in group]
    sizes = tuple(sum(x.shape[0] for x in group) for group in groups)
    rows = sum(sizes)
    tiles, count = width // tile, len(sizes)
    parts = tuple(len(group) for group in groups)
    dma = pltpu.SemaphoreType.DMA
    *res, post = pl.pallas_call(
        functools.partial(score_kernel, at=at, parts=parts, sizes=sizes, tile=tile),
        in_specs=[pl.BlockSpec(memory_space=pl.ANY)] * (len(xs) + 3),
        out_specs=[pl.BlockSpec(memory_space=pltpu.HBM)] * count + in_vmem(1),
        out_shape=[pltpu.HBM((size, width), BF) for size in sizes]
        + [jax.ShapeDtypeStruct((1, width), F32)],
        scratch_shapes=[pltpu.VMEM((size, depth), BF) for size in sizes]
        + [pltpu.VMEM((size, LANES), jnp.int32) for size in sizes]
        + [pltpu.VMEM((tiles, size, tile), BF) for size in sizes]
        + [pltpu.VMEM((tiles, tile, depth), BF), pltpu.VMEM(label.shape, F32)]
        + [dma((len(xs),)), dma((count,)), dma((tiles,)), dma(()), dma((count, tiles))],
        cost_estimate=pl.CostEstimate(
            flops=2 * rows * width * depth,
            bytes_accessed=2 * (rows * depth + width * depth + rows * width),
            transcendentals=3 * rows * width,
        ),
        compiler_params=pltpu.CompilerParams(vmem_limit_bytes=60 << 20),
        name="scores",
    )(*xs, words, w, label)
    return res, post


def weight_kernel(core_ref, *refs, count):
    x_refs, r_refs = refs[:count], refs[count:-5]
    kept_ref, given_ref, x_all, r_all, out = refs[-5:]
    mine = core_ref[0]

    @pl.when(pl.program_id(0) == 0)
    def _():
        at = 0
        for x_ref in x_refs:
            x_all[at : at + x_ref.shape[0], :] = x_ref[...]
            at += x_ref.shape[0]

    at = 0
    for r_ref in r_refs:
        r_all[at : at + r_ref.shape[0], :] = r_ref[...]
        at += r_ref.shape[0]
    out[...] = mm(x_all[...], r_all[...], ((0,), (0,))).astype(BF)
    step = kept_ref.shape[1]
    for y in range(NY):
        kept_ref[y] = out[pl.ds(pl.multiple_of((y * NC + mine) * step, step), step), :]
        given_ref[y] = out[pl.ds(pl.multiple_of((y * NC + 1 - mine) * step, step), step), :]


def weight_call(core, xs, rs, tile=512):
    depth = xs[0].shape[1]
    width = rs[0].shape[1]
    rows = sum(x.shape[0] for x in xs)
    step = depth // (NY * NC)
    half = pl.BlockSpec((NY, step, tile), lambda i: (0, 0, i))
    return pl.pallas_call(
        functools.partial(weight_kernel, count=len(xs)),
        grid=(width // tile,),
        in_specs=[pl.BlockSpec(memory_space=pltpu.SMEM)]
        + [pl.BlockSpec(x.shape, lambda i: (0, 0)) for x in xs]
        + [pl.BlockSpec((r.shape[0], tile), lambda i: (0, i)) for r in rs],
        out_specs=[half, half],
        out_shape=[pltpu.HBM((NY, step, width), BF)] * 2,
        scratch_shapes=[
            pltpu.VMEM((rows, depth), BF),
            pltpu.VMEM((rows, tile), BF),
            pltpu.VMEM((depth, tile), BF),
        ],
        cost_estimate=pl.CostEstimate(
            flops=2 * rows * width * depth,
            bytes_accessed=2 * (rows * (depth + width) + width * depth),
            transcendentals=0,
        ),
        compiler_params=pltpu.CompilerParams(vmem_limit_bytes=60 << 20),
        name="weights",
    )(core, *xs, *rs)


def shift(v, axis, n, d):
    return lax.ppermute(v, axis, ring(n, d))


def exchange(v, axis):
    return lax.all_to_all(v, axis, split_axis=0, concat_axis=0, tiled=True)


def body(
    embeddings, class_weight, class_bias, propensity, label_ids, label_count, label_bins, prior_mean
):
    width, depth = class_weight.shape
    part = embeddings.shape[0]
    block = part * NZ
    x_at, core, y = (lax.axis_index(a) for a in ("x", "core", "y"))
    offset = (x_at * NZ + lax.axis_index("z")) * width
    own = exchange(jnp.tile(embeddings, (NZ, 1)), "z")
    words, obs, label = words_call(
        jnp.stack([offset, x_at * block]),
        prior_mean,
        label_ids.T,
        label_count[None, :],
        class_bias[None, :],
        propensity[None, :],
        label_bins[None, :],
    )

    half = block // 2
    low, high = own[:half], own[half:]
    front_low, back_high = shift(low, "x", NX, -1), shift(high, "x", NX, 1)
    front_high, back_low = shift(high, "x", NX, -1), shift(low, "x", NX, 1)
    far = (shift(front_low, "x", NX, -1), shift(back_high, "x", NX, 1))
    front, back = (front_low, front_high), (back_low, back_high)
    (res0,), post0 = score_call(((own,),), (0,), words, class_weight, label)
    (res1, res3), post1 = score_call((front, back), (block, 3 * block), words, class_weight, label)
    far, post1 = lax.optimization_barrier((far, post1))
    (res2,), post2 = score_call((far,), (2 * block,), words, class_weight, label)
    post = (post0 + post1) + post2
    both = jnp.concatenate([obs, post], axis=0)[None]
    sums = jnp.sum(exchange(jnp.tile(both, (NY * NC, 1, 1)), ("y", "core")), axis=0)
    updated = ((sums[0:1] + label[2:3]) / (sums[1:2] + 8.0)).reshape(width)

    kept_rows, given = weight_call(core[None], (own, *front, *far, *back), (res0, res1, res2, res3))
    pair = kept_rows.astype(F32) + shift(given, "core", NC, 1).astype(F32)
    pair = pair.astype(BF)
    pairs = [lax.dynamic_index_in_dim(pair, (y + d) % NY, 0, keepdims=False) for d in range(NY)]

    scaled_weight = (class_weight.astype(F32) / updated[:, None]).astype(BF)

    def term(r):
        return mm(r, scaled_weight, ((1,), (0,)))

    send = lambda v, d: shift(v.astype(BF), "x", NX, d).astype(F32)
    term2 = term(res2).astype(BF)
    low2, high2 = send(term2[:half], 1), send(term2[half:], -1)
    term1 = lax.optimization_barrier(term(res1))
    term3 = lax.optimization_barrier(term(res3))
    high1, low3 = send(term1[half:], 1), send(term3[:half], -1)
    kept = term(res0)
    low1, high3 = send(term1[:half] + low2, 1), send(term3[half:] + high2, -1)
    kept, pairs = lax.optimization_barrier((kept, pairs))
    weight_sum = pairs[0].astype(F32)
    for d in (1, 2, 3):
        weight_sum = weight_sum + shift(pairs[d], "y", NY, d).astype(F32)
    weight_grad = (weight_sum / updated[None, :]).astype(BF).T

    low, high = kept[:half] + low1 + low3, kept[half:] + high1 + high3
    parts = exchange(jnp.concatenate([low, high], axis=0).astype(BF), "z")
    embed_grad = jnp.sum(parts.reshape(NZ, part, depth).astype(F32), axis=0).astype(BF)
    return updated, weight_grad, embed_grad


def solution(mesh):
    fine = Mesh(mesh.devices.reshape(NY, NC, NX, NZ), ("y", "core", "x", "z"))
    rows, labels = ("y", "core"), ("x", "z")
    both = rows + labels
    return jax.shard_map(
        body,
        mesh=fine,
        in_specs=(
            P(both, None),
            P(labels, None),
            P(labels),
            P(labels),
            P(rows, None),
            P(rows),
            P(labels),
            P(),
        ),
        out_specs=(P(labels), P(labels, rows), P(both, None)),
        check_vma=False,
    )
```

```python
import functools

import jax
import jax.numpy as jnp
from jax import lax
from jax.experimental import pallas as pl
from jax.experimental.pallas import tpu as pltpu
from jax.sharding import Mesh, PartitionSpec as P

BF = jnp.bfloat16
F32 = jnp.float32
LANES = 128
LOG2E = 1.4426950408889634
NX, NZ, NY, NC = 4, 8, 4, 2


def ring(n, d):
    return [(i, (i + d) % n) for i in range(n)]


def mm(a, b, dims):
    return lax.dot_general(a, b, (dims, ((), ())), preferred_element_type=F32)


def words_kernel(
    at_ref, mean_ref, ids_ref, count_ref, bias_ref, prop_ref, bins_ref, words_ref, obs_ref, label_ref
):
    slots, rows = ids_ref.shape
    width = bias_ref.shape[1]
    label_ref[0:1, :] = bias_ref[...] * -LOG2E
    label_ref[1:2, :] = prop_ref[...]
    bins = bins_ref[...]
    prior = jnp.zeros((1, width), F32)
    for b in range(mean_ref.shape[0]):
        prior = prior + jnp.where(bins == b, mean_ref[b], 0.0)
    label_ref[2:3, :] = 8.0 * prior
    lanes = lax.broadcasted_iota(jnp.int32, (LANES, LANES), 1)
    slot = lax.broadcasted_iota(jnp.int32, (slots, LANES), 0)
    counts = [jnp.zeros((8, LANES), jnp.int32) for _ in range(width // LANES)]
    for first in range(0, rows, LANES):
        turned = lax.rem(at_ref[1] + first, rows)
        source = pl.ds(pl.multiple_of(turned, LANES), LANES)
        local = ids_ref[:, source] - at_ref[0]
        valid = (slot < count_ref[:, source]) & (local >= 0) & (local < width)
        bit = jnp.left_shift(jnp.int32(256), jnp.where(valid, local >> 7, 0))
        code = jnp.where(valid, bit | (local & (LANES - 1)), 255).T
        words = jnp.zeros((LANES, LANES), jnp.int32)
        for i in range(slots):
            here = jnp.broadcast_to(code[:, i : i + 1], (LANES, LANES))
            words = words | jnp.where((here & 255) == lanes, here >> 8, 0)
        words_ref[first : first + LANES, :] = words
        for b in range(width // LANES):
            hit = (words >> b) & 1
            counts[b] = counts[b] + jnp.sum(hit.reshape(LANES // 8, 8, LANES), axis=0)
    for b in range(width // LANES):
        obs_ref[:, b * LANES : (b + 1) * LANES] = jnp.sum(
            counts[b].astype(F32), axis=0, keepdims=True
        )


def words_call(at, mean, ids, count, bias, prop, bins):
    rows, width = ids.shape[1], bias.shape[1]
    return pl.pallas_call(
        words_kernel,
        in_specs=[pl.BlockSpec(memory_space=pltpu.SMEM)] * 2 + in_vmem(5),
        out_specs=in_vmem(3),
        out_shape=[
            jax.ShapeDtypeStruct((rows, LANES), jnp.int32),
            jax.ShapeDtypeStruct((1, width), F32),
            jax.ShapeDtypeStruct((3, width), F32),
        ],
        cost_estimate=pl.CostEstimate(
            flops=200 * rows * LANES, bytes_accessed=8 * rows * LANES, transcendentals=0
        ),
        compiler_params=pltpu.CompilerParams(vmem_limit_bytes=16 << 20),
        name="words",
    )(at, mean, ids, count, bias, prop, bins)


def score_kernel(*refs, at, parts, sizes, tile):
    count = len(at)
    x_refs, refs = refs[: sum(parts)], refs[sum(parts) :]
    words_ref, label_ref, w_ref = refs[:3]
    res_refs, post_ref, refs = refs[3 : count + 3], refs[count + 3], refs[count + 4 :]
    x_in, words_in, slots = refs[:count], refs[count : 2 * count], refs[2 * count : 3 * count]
    label_in, x_sems, words_sems, label_sem, out_sems = refs[3 * count :]
    tiles = w_ref.shape[0] // tile

    first = []
    n = 0
    for k in range(count):
        low = 0
        for _ in range(parts[k]):
            size = x_refs[n].shape[0]
            target = x_in[k].at[low : low + size, :]
            first.append(pltpu.make_async_copy(x_refs[n], target, x_sems.at[n]))
            low, n = low + size, n + 1
        source = words_ref.at[at[k] : at[k] + sizes[k], :]
        first.append(pltpu.make_async_copy(source, words_in[k], words_sems.at[k]))
    first.append(pltpu.make_async_copy(label_ref, label_in, label_sem))
    for copy in first:
        copy.start()
    for copy in first:
        copy.wait()

    outs = []
    for t in range(tiles):
        cols = slice(t * tile, (t + 1) * tile)
        bias, prop = label_in[0:1, cols], label_in[1:2, cols]
        rest = 1.0 - prop
        total = jnp.zeros((8, tile), F32)
        for k in range(count):
            size = sizes[k]
            scores = mm(x_in[k][...], w_ref[cols, :], ((1,), (1,)))
            grown = 1.0 + jnp.exp2(scores * -LOG2E + bias)
            prob = 1.0 / grown
            unseen = rest / (grown - prop)
            words = words_in[k][...]
            bits = range(t * tile // LANES, (t + 1) * tile // LANES)
            seen = jnp.concatenate([words & (1 << b) for b in bits], axis=1)
            posterior = jnp.where(seen != 0, 1.0, unseen)
            slots[k][t] = (prob - posterior).astype(BF)
            total = total + jnp.sum(posterior.reshape(size // 8, 8, tile), axis=0)
            copy = pltpu.make_async_copy(
                slots[k].at[t], res_refs[k].at[:, cols], out_sems.at[k, t]
            )
            copy.start()
            outs.append(copy)
        post_ref[:, cols] = jnp.sum(total, axis=0, keepdims=True)
    for copy in outs:
        copy.wait()


def in_vmem(count):
    return [pl.BlockSpec(memory_space=pltpu.VMEM)] * count


def score_call(groups, at, words, w, label, tile=512):
    width, depth = w.shape
    xs = [x for group in groups for x in group]
    sizes = tuple(sum(x.shape[0] for x in group) for group in groups)
    rows = sum(sizes)
    tiles, count = width // tile, len(sizes)
    parts = tuple(len(group) for group in groups)
    dma = pltpu.SemaphoreType.DMA
    *res, post = pl.pallas_call(
        functools.partial(score_kernel, at=at, parts=parts, sizes=sizes, tile=tile),
        in_specs=[pl.BlockSpec(memory_space=pltpu.HBM)] * (len(xs) + 2) + in_vmem(1),
        out_specs=[pl.BlockSpec(memory_space=pltpu.HBM)] * count + in_vmem(1),
        out_shape=[pltpu.HBM((size, width), BF) for size in sizes]
        + [jax.ShapeDtypeStruct((1, width), F32)],
        scratch_shapes=[pltpu.VMEM((size, depth), BF) for size in sizes]
        + [pltpu.VMEM((size, LANES), jnp.int32) for size in sizes]
        + [pltpu.VMEM((tiles, size, tile), BF) for size in sizes]
        + [pltpu.VMEM(label.shape, F32)]
        + [dma((len(xs),)), dma((count,)), dma(()), dma((count, tiles))],
        cost_estimate=pl.CostEstimate(
            flops=2 * rows * width * depth,
            bytes_accessed=2 * (rows * depth + width * depth + rows * width),
            transcendentals=3 * rows * width,
        ),
        compiler_params=pltpu.CompilerParams(vmem_limit_bytes=24 << 20),
        name="scores",
    )(*xs, words, label, w)
    return res, post


def weight_kernel(core_ref, *refs, count):
    x_refs, r_refs = refs[:count], refs[count:-5]
    kept_ref, given_ref, x_all, r_all, out = refs[-5:]
    mine = core_ref[0]

    @pl.when(pl.program_id(0) == 0)
    def _():
        at = 0
        for x_ref in x_refs:
            x_all[at : at + x_ref.shape[0], :] = x_ref[...]
            at += x_ref.shape[0]

    at = 0
    for r_ref in r_refs:
        r_all[at : at + r_ref.shape[0], :] = r_ref[...]
        at += r_ref.shape[0]
    out[...] = mm(x_all[...], r_all[...], ((0,), (0,))).astype(BF)
    step = kept_ref.shape[1]
    for y in range(NY):
        kept_ref[y] = out[pl.ds(pl.multiple_of((y * NC + mine) * step, step), step), :]
        given_ref[y] = out[pl.ds(pl.multiple_of((y * NC + 1 - mine) * step, step), step), :]


def weight_call(core, xs, rs, tile=512):
    depth = xs[0].shape[1]
    width = rs[0].shape[1]
    rows = sum(x.shape[0] for x in xs)
    step = depth // (NY * NC)
    half = pl.BlockSpec((NY, step, tile), lambda i: (0, 0, i))
    return pl.pallas_call(
        functools.partial(weight_kernel, count=len(xs)),
        grid=(width // tile,),
        in_specs=[pl.BlockSpec(memory_space=pltpu.SMEM)]
        + [pl.BlockSpec(x.shape, lambda i: (0, 0)) for x in xs]
        + [pl.BlockSpec((r.shape[0], tile), lambda i: (0, i)) for r in rs],
        out_specs=[half, half],
        out_shape=[pltpu.HBM((NY, step, width), BF)] * 2,
        scratch_shapes=[
            pltpu.VMEM((rows, depth), BF),
            pltpu.VMEM((rows, tile), BF),
            pltpu.VMEM((depth, tile), BF),
        ],
        cost_estimate=pl.CostEstimate(
            flops=2 * rows * width * depth,
            bytes_accessed=2 * (rows * (depth + width) + width * depth),
            transcendentals=0,
        ),
        compiler_params=pltpu.CompilerParams(vmem_limit_bytes=60 << 20),
        name="weights",
    )(core, *xs, *rs)


def shift(v, axis, n, d):
    return lax.ppermute(v, axis, ring(n, d))


def exchange(v, axis):
    return lax.all_to_all(v, axis, split_axis=0, concat_axis=0, tiled=True)


def body(
    embeddings, class_weight, class_bias, propensity, label_ids, label_count, label_bins, prior_mean
):
    width, depth = class_weight.shape
    part = embeddings.shape[0]
    block = part * NZ
    x_at, core, y = (lax.axis_index(a) for a in ("x", "core", "y"))
    offset = (x_at * NZ + lax.axis_index("z")) * width
    own = exchange(jnp.tile(embeddings, (NZ, 1)), "z")
    words, obs, label = words_call(
        jnp.stack([offset, x_at * block]),
        prior_mean,
        label_ids.T,
        label_count[None, :],
        class_bias[None, :],
        propensity[None, :],
        label_bins[None, :],
    )

    half = block // 2
    low, high = own[:half], own[half:]
    front_low, back_high = shift(low, "x", NX, -1), shift(high, "x", NX, 1)
    front_high, back_low = shift(high, "x", NX, -1), shift(low, "x", NX, 1)
    far = (shift(front_low, "x", NX, -1), shift(back_high, "x", NX, 1))
    front, back = (front_low, front_high), (back_low, back_high)
    (res0,), post0 = score_call(((own,),), (0,), words, class_weight, label)
    (res1, res3), post1 = score_call((front, back), (block, 3 * block), words, class_weight, label)
    far, post1 = lax.optimization_barrier((far, post1))
    (res2,), post2 = score_call((far,), (2 * block,), words, class_weight, label)
    post = (post0 + post1) + post2
    both = jnp.concatenate([obs, post], axis=0)[None]
    sums = jnp.sum(exchange(jnp.tile(both, (NY * NC, 1, 1)), ("y", "core")), axis=0)
    updated = ((sums[0:1] + label[2:3]) / (sums[1:2] + 8.0)).reshape(width)

    kept_rows, given = weight_call(core[None], (own, *front, *far, *back), (res0, res1, res2, res3))
    pair = kept_rows.astype(F32) + shift(given, "core", NC, 1).astype(F32)
    pair = pair.astype(BF)
    pairs = [lax.dynamic_index_in_dim(pair, (y + d) % NY, 0, keepdims=False) for d in range(NY)]

    scaled_weight = (class_weight.astype(F32) / updated[:, None]).astype(BF)

    def term(r):
        return mm(r, scaled_weight, ((1,), (0,)))

    send = lambda v, d: shift(v.astype(BF), "x", NX, d).astype(F32)
    term2 = term(res2).astype(BF)
    low2, high2 = send(term2[:half], 1), send(term2[half:], -1)
    term1 = lax.optimization_barrier(term(res1))
    term3 = lax.optimization_barrier(term(res3))
    high1, low3 = send(term1[half:], 1), send(term3[:half], -1)
    kept = term(res0)
    low1, high3 = send(term1[:half] + low2, 1), send(term3[half:] + high2, -1)
    kept, pairs = lax.optimization_barrier((kept, pairs))
    weight_sum = pairs[0].astype(F32)
    for d in (1, 2, 3):
        weight_sum = weight_sum + shift(pairs[d], "y", NY, d).astype(F32)
    weight_grad = (weight_sum / updated[None, :]).astype(BF).T

    low, high = kept[:half] + low1 + low3, kept[half:] + high1 + high3
    parts = exchange(jnp.concatenate([low, high], axis=0).astype(BF), "z")
    embed_grad = jnp.sum(parts.reshape(NZ, part, depth).astype(F32), axis=0).astype(BF)
    return updated, weight_grad, embed_grad


def solution(mesh):
    fine = Mesh(mesh.devices.reshape(NY, NC, NX, NZ), ("y", "core", "x", "z"))
    rows, labels = ("y", "core"), ("x", "z")
    both = rows + labels
    return jax.shard_map(
        body,
        mesh=fine,
        in_specs=(
            P(both, None),
            P(labels, None),
            P(labels),
            P(labels),
            P(rows, None),
            P(rows),
            P(labels),
            P(),
        ),
        out_specs=(P(labels), P(labels, rows), P(both, None)),
        check_vma=False,
    )
```

```python
import functools

import jax
import jax.numpy as jnp
from jax import lax
from jax.experimental import pallas as pl
from jax.experimental.pallas import tpu as pltpu
from jax.sharding import Mesh, PartitionSpec as P

BF = jnp.bfloat16
F32 = jnp.float32
LANES = 128
LOG2E = 1.4426950408889634
NX, NZ, NY, NC = 4, 8, 4, 2


def ring(n, d):
    return [(i, (i + d) % n) for i in range(n)]


def mm(a, b, dims):
    return lax.dot_general(a, b, (dims, ((), ())), preferred_element_type=F32)


def words_kernel(
    at_ref, mean_ref, ids_ref, count_ref, bias_ref, prop_ref, bins_ref, words_ref, obs_ref, label_ref
):
    slots, rows = ids_ref.shape
    width = bias_ref.shape[1]
    label_ref[0:1, :] = bias_ref[...] * -LOG2E
    label_ref[1:2, :] = prop_ref[...]
    bins = bins_ref[...]
    prior = jnp.zeros((1, width), F32)
    for b in range(mean_ref.shape[0]):
        prior = prior + jnp.where(bins == b, mean_ref[b], 0.0)
    label_ref[2:3, :] = 8.0 * prior
    lanes = lax.broadcasted_iota(jnp.int32, (LANES, LANES), 1)
    slot = lax.broadcasted_iota(jnp.int32, (slots, LANES), 0)
    counts = [jnp.zeros((8, LANES), jnp.int32) for _ in range(width // LANES)]
    for first in range(0, rows, LANES):
        turned = lax.rem(at_ref[1] + first, rows)
        source = pl.ds(pl.multiple_of(turned, LANES), LANES)
        local = ids_ref[:, source] - at_ref[0]
        valid = (slot < count_ref[:, source]) & (local >= 0) & (local < width)
        bit = jnp.left_shift(jnp.int32(256), jnp.where(valid, local >> 7, 0))
        code = jnp.where(valid, bit | (local & (LANES - 1)), 255).T
        words = jnp.zeros((LANES, LANES), jnp.int32)
        for i in range(slots):
            here = jnp.broadcast_to(code[:, i : i + 1], (LANES, LANES))
            words = words | jnp.where((here & 255) == lanes, here >> 8, 0)
        words_ref[first : first + LANES, :] = words
        for b in range(width // LANES):
            hit = (words >> b) & 1
            counts[b] = counts[b] + jnp.sum(hit.reshape(LANES // 8, 8, LANES), axis=0)
    for b in range(width // LANES):
        obs_ref[:, b * LANES : (b + 1) * LANES] = jnp.sum(
            counts[b].astype(F32), axis=0, keepdims=True
        )


def words_call(at, mean, ids, count, bias, prop, bins):
    rows, width = ids.shape[1], bias.shape[1]
    return pl.pallas_call(
        words_kernel,
        in_specs=[pl.BlockSpec(memory_space=pltpu.SMEM)] * 2 + in_vmem(5),
        out_specs=in_vmem(3),
        out_shape=[
            jax.ShapeDtypeStruct((rows, LANES), jnp.int32),
            jax.ShapeDtypeStruct((1, width), F32),
            jax.ShapeDtypeStruct((3, width), F32),
        ],
        cost_estimate=pl.CostEstimate(
            flops=200 * rows * LANES, bytes_accessed=8 * rows * LANES, transcendentals=0
        ),
        compiler_params=pltpu.CompilerParams(vmem_limit_bytes=16 << 20),
        name="words",
    )(at, mean, ids, count, bias, prop, bins)


def score_kernel(*refs, at, parts, sizes, tile, stream):
    count = len(at)
    x_refs, refs = refs[: sum(parts)], refs[sum(parts) :]
    words_ref, label_ref, w_ref = refs[:3]
    res_refs, post_ref, refs = refs[3 : count + 3], refs[count + 3], refs[count + 4 :]
    x_in, words_in, slots = refs[:count], refs[count : 2 * count], refs[2 * count : 3 * count]
    label_in, total_in, x_sems, words_sems, label_sem, out_sems = refs[3 * count :][:6]
    tiles = w_ref.shape[0] // tile

    label = pltpu.make_async_copy(label_ref, label_in, label_sem)
    label.start()
    loads = []
    if stream:
        w_in, w_sems = refs[3 * count + 6 :]
        loads = [
            pltpu.make_async_copy(w_ref.at[t * tile : (t + 1) * tile, :], w_in.at[t], w_sems.at[t])
            for t in range(tiles)
        ]
    needed = []
    n = 0
    for k in range(count):
        source = words_ref.at[at[k] : at[k] + sizes[k], :]
        copies = [pltpu.make_async_copy(source, words_in[k], words_sems.at[k])]
        low = 0
        for _ in range(parts[k]):
            size = x_refs[n].shape[0]
            target = x_in[k].at[low : low + size, :]
            copies.append(pltpu.make_async_copy(x_refs[n], target, x_sems.at[n]))
            low, n = low + size, n + 1
        for copy in copies:
            copy.start()
        needed.append(copies)
        if k == 0:
            for load in loads:
                load.start()
    label.wait()

    outs = []
    for k in range(count):
        for copy in needed[k]:
            copy.wait()
        for t in range(tiles):
            cols = slice(t * tile, (t + 1) * tile)
            bias, prop = label_in[0:1, cols], label_in[1:2, cols]
            if stream and k == 0:
                loads[t].wait()
            w = w_in[t] if stream else w_ref[cols, :]
            scores = mm(x_in[k][...], w, ((1,), (1,)))
            grown = 1.0 + jnp.exp2(scores * -LOG2E + bias)
            prob = 1.0 / grown
            unseen = (1.0 - prop) / (grown - prop)
            words = words_in[k][...]
            bits = range(t * tile // LANES, (t + 1) * tile // LANES)
            seen = jnp.concatenate([words & (1 << b) for b in bits], axis=1)
            posterior = jnp.where(seen != 0, 1.0, unseen)
            slots[k][t] = (prob - posterior).astype(BF)
            total = jnp.sum(posterior.reshape(sizes[k] // 8, 8, tile), axis=0)
            total_in[:, cols] = total if k == 0 else total_in[:, cols] + total
            copy = pltpu.make_async_copy(
                slots[k].at[t], res_refs[k].at[:, cols], out_sems.at[k, t]
            )
            copy.start()
            outs.append(copy)
    post_ref[...] = jnp.sum(total_in[...], axis=0, keepdims=True)
    for copy in outs:
        copy.wait()


def in_vmem(count):
    return [pl.BlockSpec(memory_space=pltpu.VMEM)] * count


def score_call(groups, at, words, w, label, stream, tile=512):
    width, depth = w.shape
    xs = [x for group in groups for x in group]
    sizes = tuple(sum(x.shape[0] for x in group) for group in groups)
    rows = sum(sizes)
    tiles, count = width // tile, len(sizes)
    parts = tuple(len(group) for group in groups)
    dma = pltpu.SemaphoreType.DMA
    *res, post = pl.pallas_call(
        functools.partial(
            score_kernel, at=at, parts=parts, sizes=sizes, tile=tile, stream=stream
        ),
        in_specs=[pl.BlockSpec(memory_space=pltpu.HBM)] * (len(xs) + 2)
        + [pl.BlockSpec(memory_space=pltpu.HBM if stream else pltpu.VMEM)],
        out_specs=[pl.BlockSpec(memory_space=pltpu.HBM)] * count + in_vmem(1),
        out_shape=[pltpu.HBM((size, width), BF) for size in sizes]
        + [jax.ShapeDtypeStruct((1, width), F32)],
        scratch_shapes=[pltpu.VMEM((size, depth), BF) for size in sizes]
        + [pltpu.VMEM((size, LANES), jnp.int32) for size in sizes]
        + [pltpu.VMEM((tiles, size, tile), BF) for size in sizes]
        + [pltpu.VMEM(label.shape, F32), pltpu.VMEM((8, width), F32)]
        + [dma((len(xs),)), dma((count,)), dma(()), dma((count, tiles))]
        + ([pltpu.VMEM((tiles, tile, depth), BF), dma((tiles,))] if stream else []),
        cost_estimate=pl.CostEstimate(
            flops=2 * rows * width * depth,
            bytes_accessed=2 * (rows * depth + width * depth + rows * width),
            transcendentals=3 * rows * width,
        ),
        compiler_params=pltpu.CompilerParams(vmem_limit_bytes=(60 if stream else 24) << 20),
        name="scores",
    )(*xs, words, label, w)
    return res, post


def weight_kernel(core_ref, *refs, count):
    x_refs, r_refs = refs[:count], refs[count:-5]
    kept_ref, given_ref, x_all, r_all, out = refs[-5:]
    mine = core_ref[0]

    @pl.when(pl.program_id(0) == 0)
    def _():
        at = 0
        for x_ref in x_refs:
            x_all[:, at : at + x_ref.shape[0]] = x_ref[...].T
            at += x_ref.shape[0]

    at = 0
    for r_ref in r_refs:
        r_all[at : at + r_ref.shape[0], :] = r_ref[...]
        at += r_ref.shape[0]
    out[...] = mm(x_all[...], r_all[...], ((1,), (0,))).astype(BF)
    step = kept_ref.shape[1]
    for y in range(NY):
        kept_ref[y] = out[pl.ds(pl.multiple_of((y * NC + mine) * step, step), step), :]
        given_ref[y] = out[pl.ds(pl.multiple_of((y * NC + 1 - mine) * step, step), step), :]


def weight_call(core, xs, rs, tile=512):
    depth = xs[0].shape[1]
    width = rs[0].shape[1]
    rows = sum(x.shape[0] for x in xs)
    step = depth // (NY * NC)
    half = pl.BlockSpec((NY, step, tile), lambda i: (0, 0, i))
    return pl.pallas_call(
        functools.partial(weight_kernel, count=len(xs)),
        grid=(width // tile,),
        in_specs=[pl.BlockSpec(memory_space=pltpu.SMEM)]
        + [pl.BlockSpec(x.shape, lambda i: (0, 0)) for x in xs]
        + [pl.BlockSpec((r.shape[0], tile), lambda i: (0, i)) for r in rs],
        out_specs=[half, half],
        out_shape=[pltpu.HBM((NY, step, width), BF)] * 2,
        scratch_shapes=[
            pltpu.VMEM((depth, rows), BF),
            pltpu.VMEM((rows, tile), BF),
            pltpu.VMEM((depth, tile), BF),
        ],
        cost_estimate=pl.CostEstimate(
            flops=2 * rows * width * depth,
            bytes_accessed=2 * (rows * (depth + width) + width * depth),
            transcendentals=0,
        ),
        compiler_params=pltpu.CompilerParams(vmem_limit_bytes=60 << 20),
        name="weights",
    )(core, *xs, *rs)


def shift(v, axis, n, d):
    return lax.ppermute(v, axis, ring(n, d))


def exchange(v, axis):
    return lax.all_to_all(v, axis, split_axis=0, concat_axis=0, tiled=True)


def body(
    embeddings, class_weight, class_bias, propensity, label_ids, label_count, label_bins, prior_mean
):
    width, depth = class_weight.shape
    part = embeddings.shape[0]
    block = part * NZ
    x_at, core, y = (lax.axis_index(a) for a in ("x", "core", "y"))
    offset = (x_at * NZ + lax.axis_index("z")) * width
    own = exchange(jnp.tile(embeddings, (NZ, 1)), "z")
    words, obs, label = words_call(
        jnp.stack([offset, x_at * block]),
        prior_mean,
        label_ids.T,
        label_count[None, :],
        class_bias[None, :],
        propensity[None, :],
        label_bins[None, :],
    )

    half = block // 2
    low, high = own[:half], own[half:]
    front_low, back_high = shift(low, "x", NX, -1), shift(high, "x", NX, 1)
    front_high, back_low = shift(high, "x", NX, -1), shift(low, "x", NX, 1)
    far = (shift(front_low, "x", NX, -1), shift(back_high, "x", NX, 1))
    front, back = (front_low, front_high), (back_low, back_high)
    (res0, res1, res3), post1 = score_call(
        ((own,), front, back), (0, block, 3 * block), words, class_weight, label, True
    )
    far, post1 = lax.optimization_barrier((far, post1))
    (res2,), post2 = score_call((far,), (2 * block,), words, class_weight, label, False)
    post = post1 + post2
    both = jnp.concatenate([obs, post], axis=0)[None]
    sums = jnp.sum(exchange(jnp.tile(both, (NY * NC, 1, 1)), ("y", "core")), axis=0)
    updated = ((sums[0:1] + label[2:3]) / (sums[1:2] + 8.0)).reshape(width)

    kept_rows, given = weight_call(core[None], (own, *front, *far, *back), (res0, res1, res2, res3))
    pair = kept_rows.astype(F32) + shift(given, "core", NC, 1).astype(F32)
    pair = pair.astype(BF)
    pairs = [lax.dynamic_index_in_dim(pair, (y + d) % NY, 0, keepdims=False) for d in range(NY)]

    scaled_weight = (class_weight.astype(F32) / updated[:, None]).astype(BF)

    def term(r):
        return mm(r, scaled_weight, ((1,), (0,)))

    send = lambda v, d: shift(v.astype(BF), "x", NX, d).astype(F32)
    term2 = term(res2).astype(BF)
    low2, high2 = send(term2[:half], 1), send(term2[half:], -1)
    term1 = lax.optimization_barrier(term(res1))
    term3 = lax.optimization_barrier(term(res3))
    high1, low3 = send(term1[half:], 1), send(term3[:half], -1)
    kept = term(res0)
    low1, high3 = send(term1[:half] + low2, 1), send(term3[half:] + high2, -1)
    kept, pairs = lax.optimization_barrier((kept, pairs))
    weight_sum = pairs[0].astype(F32)
    for d in (1, 2, 3):
        weight_sum = weight_sum + shift(pairs[d], "y", NY, d).astype(F32)
    weight_grad = (weight_sum / updated[None, :]).astype(BF).T

    low, high = kept[:half] + low1 + low3, kept[half:] + high1 + high3
    parts = exchange(jnp.concatenate([low, high], axis=0).astype(BF), "z")
    embed_grad = jnp.sum(parts.reshape(NZ, part, depth).astype(F32), axis=0).astype(BF)
    return updated, weight_grad, embed_grad


def solution(mesh):
    fine = Mesh(mesh.devices.reshape(NY, NC, NX, NZ), ("y", "core", "x", "z"))
    rows, labels = ("y", "core"), ("x", "z")
    both = rows + labels
    return jax.shard_map(
        body,
        mesh=fine,
        in_specs=(
            P(both, None),
            P(labels, None),
            P(labels),
            P(labels),
            P(rows, None),
            P(rows),
            P(labels),
            P(),
        ),
        out_specs=(P(labels), P(labels, rows), P(both, None)),
        check_vma=False,
    )
```

```python
import functools

import jax
import jax.numpy as jnp
from jax import lax
from jax.experimental import pallas as pl
from jax.experimental.pallas import tpu as pltpu
from jax.sharding import Mesh, PartitionSpec as P

BF = jnp.bfloat16
F32 = jnp.float32
LANES = 128
LOG2E = 1.4426950408889634
NX, NZ, NY, NC = 4, 8, 4, 2


def ring(n, d):
    return [(i, (i + d) % n) for i in range(n)]


def mm(a, b, dims):
    return lax.dot_general(a, b, (dims, ((), ())), preferred_element_type=F32)


def words_kernel(
    at_ref, mean_ref, ids_ref, count_ref, bias_ref, prop_ref, bins_ref, words_ref, obs_ref, label_ref
):
    slots, rows = ids_ref.shape
    width = bias_ref.shape[1]
    label_ref[0:1, :] = bias_ref[...] * -LOG2E
    label_ref[1:2, :] = prop_ref[...]
    bins = bins_ref[...]
    prior = jnp.zeros((1, width), F32)
    for b in range(mean_ref.shape[0]):
        prior = prior + jnp.where(bins == b, mean_ref[b], 0.0)
    label_ref[2:3, :] = 8.0 * prior
    lanes = lax.broadcasted_iota(jnp.int32, (LANES, LANES), 1)
    slot = lax.broadcasted_iota(jnp.int32, (slots, LANES), 0)
    counts = [jnp.zeros((8, LANES), jnp.int32) for _ in range(width // LANES)]
    for first in range(0, rows, LANES):
        turned = lax.rem(at_ref[1] + first, rows)
        source = pl.ds(pl.multiple_of(turned, LANES), LANES)
        local = ids_ref[:, source] - at_ref[0]
        valid = (slot < count_ref[:, source]) & (local >= 0) & (local < width)
        bit = jnp.left_shift(jnp.int32(256), jnp.where(valid, local >> 7, 0))
        code = jnp.where(valid, bit | (local & (LANES - 1)), 255).T
        words = jnp.zeros((LANES, LANES), jnp.int32)
        for i in range(slots):
            here = jnp.broadcast_to(code[:, i : i + 1], (LANES, LANES))
            words = words | jnp.where((here & 255) == lanes, here >> 8, 0)
        words_ref[first : first + LANES, :] = words
        for b in range(width // LANES):
            hit = (words >> b) & 1
            counts[b] = counts[b] + jnp.sum(hit.reshape(LANES // 8, 8, LANES), axis=0)
    for b in range(width // LANES):
        obs_ref[:, b * LANES : (b + 1) * LANES] = jnp.sum(
            counts[b].astype(F32), axis=0, keepdims=True
        )


def words_call(at, mean, ids, count, bias, prop, bins):
    rows, width = ids.shape[1], bias.shape[1]
    return pl.pallas_call(
        words_kernel,
        in_specs=[pl.BlockSpec(memory_space=pltpu.SMEM)] * 2 + in_vmem(5),
        out_specs=in_vmem(3),
        out_shape=[
            jax.ShapeDtypeStruct((rows, LANES), jnp.int32),
            jax.ShapeDtypeStruct((1, width), F32),
            jax.ShapeDtypeStruct((3, width), F32),
        ],
        cost_estimate=pl.CostEstimate(
            flops=200 * rows * LANES, bytes_accessed=8 * rows * LANES, transcendentals=0
        ),
        compiler_params=pltpu.CompilerParams(vmem_limit_bytes=16 << 20),
        name="words",
    )(at, mean, ids, count, bias, prop, bins)


def score_kernel(*refs, at, parts, tile):
    count = len(at)
    x_refs, refs = refs[: sum(parts)], refs[sum(parts) :]
    words_ref, w_ref, label_ref = refs[:3]
    res_refs, post_ref = refs[3 : count + 3], refs[count + 3]
    slots, sems = refs[count + 4 : 2 * count + 4], refs[2 * count + 4]
    starts = [sum(parts[:k]) for k in range(count)]
    blocks = [x_refs[s : s + p] for s, p in zip(starts, parts)]
    copies = []
    for t in range(w_ref.shape[0] // tile):
        cols = slice(t * tile, (t + 1) * tile)
        bias, prop = label_ref[0:1, cols], label_ref[1:2, cols]
        rest = 1.0 - prop
        total = jnp.zeros((8, tile), F32)
        for k in range(count):
            x = jnp.concatenate([x_ref[...] for x_ref in blocks[k]], axis=0)
            size = x.shape[0]
            scores = mm(x, w_ref[cols, :], ((1,), (1,)))
            grown = 1.0 + jnp.exp2(scores * -LOG2E + bias)
            prob = 1.0 / grown
            unseen = rest / (grown - prop)
            words = words_ref[at[k] : at[k] + size, :]
            bits = range(t * tile // LANES, (t + 1) * tile // LANES)
            seen = jnp.concatenate([words & (1 << b) for b in bits], axis=1)
            posterior = jnp.where(seen != 0, 1.0, unseen)
            slots[k][t] = (prob - posterior).astype(BF)
            total = total + jnp.sum(posterior.reshape(size // 8, 8, tile), axis=0)
            copy = pltpu.make_async_copy(slots[k].at[t], res_refs[k].at[:, cols], sems.at[k, t])
            copy.start()
            copies.append(copy)
        post_ref[:, cols] = jnp.sum(total, axis=0, keepdims=True)
    for copy in copies:
        copy.wait()


def in_vmem(count):
    return [pl.BlockSpec(memory_space=pltpu.VMEM)] * count


def score_call(groups, at, words, w, label, tile=512):
    width, depth = w.shape
    xs = [x for group in groups for x in group]
    sizes = [sum(x.shape[0] for x in group) for group in groups]
    rows = sum(sizes)
    tiles = width // tile
    parts = tuple(len(group) for group in groups)
    *res, post = pl.pallas_call(
        functools.partial(score_kernel, at=at, parts=parts, tile=tile),
        in_specs=in_vmem(len(xs) + 3),
        out_specs=[pl.BlockSpec(memory_space=pltpu.HBM)] * len(sizes) + in_vmem(1),
        out_shape=[pltpu.HBM((size, width), BF) for size in sizes]
        + [jax.ShapeDtypeStruct((1, width), F32)],
        scratch_shapes=[pltpu.VMEM((tiles, size, tile), BF) for size in sizes]
        + [pltpu.SemaphoreType.DMA((len(sizes), tiles))],
        cost_estimate=pl.CostEstimate(
            flops=2 * rows * width * depth,
            bytes_accessed=2 * (rows * depth + width * depth + rows * width),
            transcendentals=3 * rows * width,
        ),
        compiler_params=pltpu.CompilerParams(vmem_limit_bytes=24 << 20),
        name="scores",
    )(*xs, words, w, label)
    return res, post


def weight_kernel(core_ref, *refs, count):
    x_refs, r_refs = refs[:count], refs[count:-5]
    kept_ref, given_ref, x_all, r_all, out = refs[-5:]
    mine = core_ref[0]

    @pl.when(pl.program_id(0) == 0)
    def _():
        at = 0
        for x_ref in x_refs:
            x_all[at : at + x_ref.shape[0], :] = x_ref[...]
            at += x_ref.shape[0]

    at = 0
    for r_ref in r_refs:
        r_all[at : at + r_ref.shape[0], :] = r_ref[...]
        at += r_ref.shape[0]
    out[...] = mm(x_all[...], r_all[...], ((0,), (0,))).astype(BF)
    step = kept_ref.shape[1]
    for y in range(NY):
        kept_ref[y] = out[pl.ds(pl.multiple_of((y * NC + mine) * step, step), step), :]
        given_ref[y] = out[pl.ds(pl.multiple_of((y * NC + 1 - mine) * step, step), step), :]


def weight_call(core, xs, rs, tile=512):
    depth = xs[0].shape[1]
    width = rs[0].shape[1]
    rows = sum(x.shape[0] for x in xs)
    step = depth // (NY * NC)
    half = pl.BlockSpec((NY, step, tile), lambda i: (0, 0, i))
    return pl.pallas_call(
        functools.partial(weight_kernel, count=len(xs)),
        grid=(width // tile,),
        in_specs=[pl.BlockSpec(memory_space=pltpu.SMEM)]
        + [pl.BlockSpec(x.shape, lambda i: (0, 0)) for x in xs]
        + [pl.BlockSpec((r.shape[0], tile), lambda i: (0, i)) for r in rs],
        out_specs=[half, half],
        out_shape=[pltpu.HBM((NY, step, width), BF)] * 2,
        scratch_shapes=[
            pltpu.VMEM((rows, depth), BF),
            pltpu.VMEM((rows, tile), BF),
            pltpu.VMEM((depth, tile), BF),
        ],
        cost_estimate=pl.CostEstimate(
            flops=2 * rows * width * depth,
            bytes_accessed=2 * (rows * (depth + width) + width * depth),
            transcendentals=0,
        ),
        compiler_params=pltpu.CompilerParams(vmem_limit_bytes=60 << 20),
        name="weights",
    )(core, *xs, *rs)


def shift(v, axis, n, d):
    return lax.ppermute(v, axis, ring(n, d))


def exchange(v, axis):
    return lax.all_to_all(v, axis, split_axis=0, concat_axis=0, tiled=True)


def body(
    embeddings, class_weight, class_bias, propensity, label_ids, label_count, label_bins, prior_mean
):
    width, depth = class_weight.shape
    part = embeddings.shape[0]
    block = part * NZ
    x_at, core, y = (lax.axis_index(a) for a in ("x", "core", "y"))
    offset = (x_at * NZ + lax.axis_index("z")) * width

    own = exchange(jnp.tile(embeddings, (NZ, 1)), "z")
    words, obs, label = words_call(
        jnp.stack([offset, x_at * block]),
        prior_mean,
        label_ids.T,
        label_count[None, :],
        class_bias[None, :],
        propensity[None, :],
        label_bins[None, :],
    )

    half = block // 2
    front, back = shift(own, "x", NX, -1), shift(own, "x", NX, 1)
    far = (shift(front[:half], "x", NX, -1), shift(back[half:], "x", NX, 1))
    (res0,), post0 = score_call(((own,),), (0,), words, class_weight, label)
    (res1, res3), post1 = score_call(
        ((front,), (back,)), (block, 3 * block), words, class_weight, label
    )
    far, post1 = lax.optimization_barrier((far, post1))
    (res2,), post2 = score_call((far,), (2 * block,), words, class_weight, label)
    post = (post0 + post1) + post2
    both = jnp.concatenate([obs, post], axis=0)[None]
    sums = jnp.sum(exchange(jnp.tile(both, (NY * NC, 1, 1)), ("y", "core")), axis=0)
    updated = ((sums[0:1] + label[2:3]) / (sums[1:2] + 8.0)).reshape(width)

    kept_rows, given = weight_call(core[None], (own, front, *far, back), (res0, res1, res2, res3))
    pair = kept_rows.astype(F32) + shift(given, "core", NC, 1).astype(F32)
    pair = pair.astype(BF)
    pairs = [lax.dynamic_index_in_dim(pair, (y + d) % NY, 0, keepdims=False) for d in range(NY)]

    scaled_weight = (class_weight.astype(F32) / updated[:, None]).astype(BF)

    def term(r):
        return mm(r, scaled_weight, ((1,), (0,)))

    send = lambda v, d: shift(v.astype(BF), "x", NX, d).astype(F32)
    term2 = term(res2).astype(BF)
    low2, high2 = send(term2[:half], 1), send(term2[half:], -1)
    term1 = lax.optimization_barrier(term(res1))
    term3 = lax.optimization_barrier(term(res3))
    high1, low3 = send(term1[half:], 1), send(term3[:half], -1)
    kept = term(res0)
    low1, high3 = send(term1[:half] + low2, 1), send(term3[half:] + high2, -1)
    kept, pairs = lax.optimization_barrier((kept, pairs))
    weight_sum = pairs[0].astype(F32)
    for d in (1, 2, 3):
        weight_sum = weight_sum + shift(pairs[d], "y", NY, d).astype(F32)
    weight_grad = (weight_sum / updated[None, :]).astype(BF).T

    low, high = kept[:half] + low1 + low3, kept[half:] + high1 + high3
    parts = exchange(jnp.concatenate([low, high], axis=0).astype(BF), "z")
    embed_grad = jnp.sum(parts.reshape(NZ, part, depth).astype(F32), axis=0).astype(BF)
    return updated, weight_grad, embed_grad


def solution(mesh):
    fine = Mesh(mesh.devices.reshape(NY, NC, NX, NZ), ("y", "core", "x", "z"))
    rows, labels = ("y", "core"), ("x", "z")
    both = rows + labels
    return jax.shard_map(
        body,
        mesh=fine,
        in_specs=(
            P(both, None),
            P(labels, None),
            P(labels),
            P(labels),
            P(rows, None),
            P(rows),
            P(labels),
            P(),
        ),
        out_specs=(P(labels), P(labels, rows), P(both, None)),
        check_vma=False,
    )
```

```python
import functools

import jax
import jax.numpy as jnp
from jax import lax
from jax.experimental import pallas as pl
from jax.experimental.pallas import tpu as pltpu
from jax.sharding import Mesh, PartitionSpec as P

BF = jnp.bfloat16
F32 = jnp.float32
LANES = 128
LOG2E = 1.4426950408889634
NX, NZ, NY, NC = 4, 8, 4, 2


def ring(n, d):
    return [(i, (i + d) % n) for i in range(n)]


def mm(a, b, dims):
    return lax.dot_general(a, b, (dims, ((), ())), preferred_element_type=F32)


def words_kernel(at_ref, ids_ref, count_ref, _, words_ref, obs_ref, *, width):
    slots, rows = ids_ref.shape
    lanes = lax.broadcasted_iota(jnp.int32, (LANES, LANES), 1)
    slot = lax.broadcasted_iota(jnp.int32, (slots, LANES), 0)
    counts = [jnp.zeros((8, LANES), jnp.int32) for _ in range(width // LANES)]
    for first in range(0, rows, LANES):
        turned = lax.rem(at_ref[1] + first, rows)
        source = pl.ds(pl.multiple_of(turned, LANES), LANES)
        local = ids_ref[:, source] - at_ref[0]
        valid = (slot < count_ref[:, source]) & (local >= 0) & (local < width)
        bit = jnp.left_shift(jnp.int32(256), jnp.where(valid, local >> 7, 0))
        code = jnp.where(valid, bit | (local & (LANES - 1)), 255).T
        words = jnp.zeros((LANES, LANES), jnp.int32)
        for i in range(slots):
            here = jnp.broadcast_to(code[:, i : i + 1], (LANES, LANES))
            words = words | jnp.where((here & 255) == lanes, here >> 8, 0)
        words_ref[first : first + LANES, :] = words
        for b in range(width // LANES):
            hit = (words >> b) & 1
            counts[b] = counts[b] + jnp.sum(hit.reshape(LANES // 8, 8, LANES), axis=0)
    for b in range(width // LANES):
        obs_ref[:, b * LANES : (b + 1) * LANES] = jnp.sum(
            counts[b].astype(F32), axis=0, keepdims=True
        )


def words_call(at, ids, count, w):
    width = w.shape[0]
    rows = ids.shape[1]
    return pl.pallas_call(
        functools.partial(words_kernel, width=width),
        in_specs=[pl.BlockSpec(memory_space=pltpu.SMEM)] + in_vmem(3),
        out_specs=in_vmem(2),
        out_shape=[
            jax.ShapeDtypeStruct((rows, LANES), jnp.int32),
            jax.ShapeDtypeStruct((1, width), F32),
        ],
        cost_estimate=pl.CostEstimate(
            flops=200 * rows * LANES, bytes_accessed=8 * rows * LANES, transcendentals=0
        ),
        compiler_params=pltpu.CompilerParams(vmem_limit_bytes=16 << 20),
        name="words",
    )(at, ids, count, w)


def score_kernel(*refs, at, parts, tile):
    count = len(at)
    x_refs, refs = refs[: sum(parts)], refs[sum(parts) :]
    words_ref, w_ref, bias_ref, prop_ref = refs[:4]
    res_refs, post_ref = refs[4 : count + 4], refs[count + 4]
    slots, sems = refs[count + 5 : 2 * count + 5], refs[2 * count + 5]
    starts = [sum(parts[:k]) for k in range(count)]
    blocks = [x_refs[s : s + p] for s, p in zip(starts, parts)]
    copies = []
    for t in range(w_ref.shape[0] // tile):
        cols = slice(t * tile, (t + 1) * tile)
        bias = bias_ref[:, cols] * -LOG2E
        prop = prop_ref[:, cols]
        rest = 1.0 - prop
        total = jnp.zeros((8, tile), F32)
        for k in range(count):
            x = jnp.concatenate([x_ref[...] for x_ref in blocks[k]], axis=0)
            size = x.shape[0]
            scores = mm(x, w_ref[cols, :], ((1,), (1,)))
            grown = 1.0 + jnp.exp2(scores * -LOG2E + bias)
            prob = 1.0 / grown
            unseen = rest / (grown - prop)
            words = words_ref[at[k] : at[k] + size, :]
            bits = range(t * tile // LANES, (t + 1) * tile // LANES)
            seen = jnp.concatenate([words & (1 << b) for b in bits], axis=1)
            posterior = jnp.where(seen != 0, 1.0, unseen)
            slots[k][t] = (prob - posterior).astype(BF)
            total = total + jnp.sum(posterior.reshape(size // 8, 8, tile), axis=0)
            copy = pltpu.make_async_copy(slots[k].at[t], res_refs[k].at[:, cols], sems.at[k, t])
            copy.start()
            copies.append(copy)
        post_ref[:, cols] = jnp.sum(total, axis=0, keepdims=True)
    for copy in copies:
        copy.wait()


def in_vmem(count):
    return [pl.BlockSpec(memory_space=pltpu.VMEM)] * count


def score_call(groups, at, words, w, bias, prop, tile=512):
    width, depth = w.shape
    xs = [x for group in groups for x in group]
    sizes = [sum(x.shape[0] for x in group) for group in groups]
    rows = sum(sizes)
    tiles = width // tile
    parts = tuple(len(group) for group in groups)
    *res, post = pl.pallas_call(
        functools.partial(score_kernel, at=at, parts=parts, tile=tile),
        in_specs=in_vmem(len(xs) + 4),
        out_specs=[pl.BlockSpec(memory_space=pltpu.HBM)] * len(sizes) + in_vmem(1),
        out_shape=[pltpu.HBM((size, width), BF) for size in sizes]
        + [jax.ShapeDtypeStruct((1, width), F32)],
        scratch_shapes=[pltpu.VMEM((tiles, size, tile), BF) for size in sizes]
        + [pltpu.SemaphoreType.DMA((len(sizes), tiles))],
        cost_estimate=pl.CostEstimate(
            flops=2 * rows * width * depth,
            bytes_accessed=2 * (rows * depth + width * depth + rows * width),
            transcendentals=3 * rows * width,
        ),
        compiler_params=pltpu.CompilerParams(vmem_limit_bytes=24 << 20),
        name="scores",
    )(*xs, words, w, bias, prop)
    return res, post


def weight_kernel(core_ref, *refs, count):
    x_refs, r_refs = refs[:count], refs[count:-5]
    kept_ref, given_ref, x_all, r_all, out = refs[-5:]
    mine = core_ref[0]

    @pl.when(pl.program_id(0) == 0)
    def _():
        at = 0
        for x_ref in x_refs:
            x_all[at : at + x_ref.shape[0], :] = x_ref[...]
            at += x_ref.shape[0]

    at = 0
    for r_ref in r_refs:
        r_all[at : at + r_ref.shape[0], :] = r_ref[...]
        at += r_ref.shape[0]
    out[...] = mm(x_all[...], r_all[...], ((0,), (0,))).astype(BF)
    step = kept_ref.shape[1]
    for y in range(NY):
        kept_ref[y] = out[pl.ds(pl.multiple_of((y * NC + mine) * step, step), step), :]
        given_ref[y] = out[pl.ds(pl.multiple_of((y * NC + 1 - mine) * step, step), step), :]


def weight_call(core, xs, rs, tile=512):
    depth = xs[0].shape[1]
    width = rs[0].shape[1]
    rows = sum(x.shape[0] for x in xs)
    step = depth // (NY * NC)
    half = pl.BlockSpec((NY, step, tile), lambda i: (0, 0, i))
    return pl.pallas_call(
        functools.partial(weight_kernel, count=len(xs)),
        grid=(width // tile,),
        in_specs=[pl.BlockSpec(memory_space=pltpu.SMEM)]
        + [pl.BlockSpec(x.shape, lambda i: (0, 0)) for x in xs]
        + [pl.BlockSpec((r.shape[0], tile), lambda i: (0, i)) for r in rs],
        out_specs=[half, half],
        out_shape=[pltpu.HBM((NY, step, width), BF)] * 2,
        scratch_shapes=[
            pltpu.VMEM((rows, depth), BF),
            pltpu.VMEM((rows, tile), BF),
            pltpu.VMEM((depth, tile), BF),
        ],
        cost_estimate=pl.CostEstimate(
            flops=2 * rows * width * depth,
            bytes_accessed=2 * (rows * (depth + width) + width * depth),
            transcendentals=0,
        ),
        compiler_params=pltpu.CompilerParams(vmem_limit_bytes=60 << 20),
        name="weights",
    )(core, *xs, *rs)


def bin_prior(bins, prior_mean):
    levels = jnp.arange(prior_mean.shape[0], dtype=jnp.int32)
    onehot = (bins[:, None] == levels[None, :]).astype(F32)
    return jnp.sum(onehot * prior_mean[None, :], axis=1)


def shift(v, axis, n, d):
    return lax.ppermute(v, axis, ring(n, d))


def exchange(v, axis):
    return lax.all_to_all(v, axis, split_axis=0, concat_axis=0, tiled=True)


def body(
    embeddings, class_weight, class_bias, propensity, label_ids, label_count, label_bins, prior_mean
):
    width, depth = class_weight.shape
    part = embeddings.shape[0]
    block = part * NZ
    x_at, core, y = (lax.axis_index(a) for a in ("x", "core", "y"))
    offset = (x_at * NZ + lax.axis_index("z")) * width
    bias, prop = class_bias[None, :], propensity[None, :]

    own = exchange(jnp.tile(embeddings, (NZ, 1)), "z")
    at = jnp.stack([offset, x_at * block])
    words, obs = words_call(at, label_ids.T, label_count[None, :], class_weight)
    prior = bin_prior(label_bins, prior_mean)

    half = block // 2
    front, back = shift(own, "x", NX, -1), shift(own, "x", NX, 1)
    far = (shift(front[:half], "x", NX, -1), shift(back[half:], "x", NX, 1))
    (res0,), post0 = score_call(((own,),), (0,), words, class_weight, bias, prop)
    (res1, res3), post1 = score_call(
        ((front,), (back,)), (block, 3 * block), words, class_weight, bias, prop
    )
    far, post1 = lax.optimization_barrier((far, post1))
    (res2,), post2 = score_call((far,), (2 * block,), words, class_weight, bias, prop)
    post = (post0 + post1) + post2
    both = jnp.concatenate([obs, post], axis=0)[None]
    sums = jnp.sum(exchange(jnp.tile(both, (NY * NC, 1, 1)), ("y", "core")), axis=0)
    updated = ((sums[0:1] + 8.0 * prior[None, :]) / (sums[1:2] + 8.0)).reshape(width)

    kept_rows, given = weight_call(core[None], (own, front, *far, back), (res0, res1, res2, res3))
    pair = kept_rows.astype(F32) + shift(given, "core", NC, 1).astype(F32)
    pair = pair.astype(BF)
    pairs = [lax.dynamic_index_in_dim(pair, (y + d) % NY, 0, keepdims=False) for d in range(NY)]

    scaled_weight = (class_weight.astype(F32) / updated[:, None]).astype(BF)

    def term(r):
        return mm(r, scaled_weight, ((1,), (0,)))

    send = lambda v, d: shift(v.astype(BF), "x", NX, d).astype(F32)
    term2 = term(res2).astype(BF)
    low2, high2 = send(term2[:half], 1), send(term2[half:], -1)
    term1 = lax.optimization_barrier(term(res1))
    term3 = lax.optimization_barrier(term(res3))
    high1, low3 = send(term1[half:], 1), send(term3[:half], -1)
    kept = term(res0)
    low1, high3 = send(term1[:half] + low2, 1), send(term3[half:] + high2, -1)
    kept, pairs = lax.optimization_barrier((kept, pairs))
    weight_sum = pairs[0].astype(F32)
    for d in (1, 2, 3):
        weight_sum = weight_sum + shift(pairs[d], "y", NY, d).astype(F32)
    weight_grad = (weight_sum / updated[None, :]).astype(BF).T

    low, high = kept[:half] + low1 + low3, kept[half:] + high1 + high3
    parts = exchange(jnp.concatenate([low, high], axis=0).astype(BF), "z")
    embed_grad = jnp.sum(parts.reshape(NZ, part, depth).astype(F32), axis=0).astype(BF)
    return updated, weight_grad, embed_grad


def solution(mesh):
    fine = Mesh(mesh.devices.reshape(NY, NC, NX, NZ), ("y", "core", "x", "z"))
    rows, labels = ("y", "core"), ("x", "z")
    both = rows + labels
    return jax.shard_map(
        body,
        mesh=fine,
        in_specs=(
            P(both, None),
            P(labels, None),
            P(labels),
            P(labels),
            P(rows, None),
            P(rows),
            P(labels),
            P(),
        ),
        out_specs=(P(labels), P(labels, rows), P(both, None)),
        check_vma=False,
    )
```
